256 devices in a mesh: grp: 8 (over z), sl: 32 (over y, x, core).
Axes of the slice: x: 4, y: 4, z: 8, core: 2. Of those that a mesh axis runs over, the one named last changes fastest.
Arguments:
- radiation: float32 [512, 128, 2, 128], P(('grp', 'sl')), may hold values from -6 to 6
- phases: float32 [512, 4096], P(('grp', 'sl')), may hold values from -3.140625 to 3.140625
- energies: float32 [512, 4096], P(('grp', 'sl')), may hold values from -4 to 4
- cell_row: int32 [512, 4096], P(('grp', 'sl')), may hold values from 0 to 127
- cell_col: int32 [512, 4096], P(('grp', 'sl')), may hold values from 0 to 127
- landing: int32 [16384, 1], P(('grp', 'sl')), may hold values from 0 to 31; in each aligned block of 64 rows (0 to 63, 64 to 127, ...) at most 4 rows name the same one
Outputs:
- radiation_out: float32 [512, 128, 2, 128], P(('grp', 'sl'))
- bunching: float32 [512, 128, 2, 128], P(('grp', 'sl'))
The draws below stay inside these ranges and needn't reach their ends.
Inputs may be any that keep to these rules, and one draw needn't show every extreme that they name: `landing`: among the 64 blocks of one device (aligned runs of 64 blocks), no value occurs more than 4 times, and some value occurs exactly 4 times in some such run.
All inputs are finite; a program needn't handle non-finite values.
Results may differ from the reference program's by a relative error of at most 0.0065.
The reference program's roundings to bfloat16 on the way count: a program that leaves them out, or rounds other values in their place, can miss the bound.
Values sent between devices are 32-bit elements; how exact they have to be, the bound alone decides.
A program may use at most 64 MiB of HBM per device.

```python
import math
import jax
import jax.numpy as jnp
import numpy as np
from jax import lax

GRID = 128
S_DEV = 2
NE = 4096
STEPS = 8
EBLK = 128
BLK_DEV = 64
MOST = 4
SLICES = 512
BLOCKS = 16384
N_SL = 32


def plant(result, rng, low, top_value):
    spot = [jax.random.randint(jax.random.fold_in(rng, axis), (), 0, length) for axis, length in enumerate(result.shape)]
    main_axis = result.shape.index(max(result.shape))
    beside = spot[:main_axis] + [(spot[main_axis] + 1) % result.shape[main_axis]] + spot[main_axis + 1:]
    return result.at[tuple(spot)].set(low).at[tuple(beside)].set(top_value)


def level_of(stream_key, shape, cuts, smallest, high):
    loudness = 1.0
    for position, shards_of in cuts:
        steps = jax.random.uniform(jax.random.fold_in(jax.random.fold_in(stream_key, 6), position), (shards_of,), jnp.float32, smallest / len(cuts), high / len(cuts))
        loudness = loudness * jnp.repeat(jnp.exp(steps), shape[position] // shards_of).reshape((-1,) + (1,) * (len(shape) - 1 - position))
    return loudness


def assign_block(key, own, number, rows, number_of, top, bound, slope):
    sequence = jax.random.permutation(key, number_of)
    crowded, usual = shares(number_of, rows * top, bound, slope, True), shares(number_of, rows * top, bound, slope, False)
    places = jnp.arange(number_of)

    def named(tallies, rotation):
        used = int((tallies > 0).sum())
        fixed = max(1, used // 4)
        passed = fixed + (places - fixed + rotation * (used - fixed)) % max(1, number_of - fixed)
        return jnp.zeros((number_of,), jnp.int32).at[sequence[jnp.where(places < fixed, places, passed)]].set(jnp.asarray(tallies, jnp.int32))

    tallies = jnp.where(number % 4 == 0, named(crowded, number // 4), named(usual, number - number // 4 - 1))
    mixed = jax.random.permutation(jax.random.fold_in(own, 3), number_of)
    source_of, receiver = mixed[0:number_of // 2 * 2:2], mixed[1:number_of // 2 * 2:2]
    room = jnp.minimum(tallies[source_of] - 1, bound - tallies[receiver]) // 2
    room = jnp.where((source_of == sequence[0]) | (receiver == sequence[0]) | (tallies[receiver] == 0), 0, jnp.maximum(room, 0))
    passed = jax.random.randint(jax.random.fold_in(own, 4), (number_of // 2,), 0, 1 << 20) % (room + 1)
    tallies = tallies.at[source_of].add(-passed).at[receiver].add(passed)
    items = jnp.searchsorted(jnp.cumsum(tallies), jnp.arange(rows * top), side="right").astype(jnp.int32)
    listing = items.reshape(top, rows).T
    listing = listing[jax.random.permutation(jax.random.fold_in(own, 1), rows)]
    rotation = jax.random.randint(jax.random.fold_in(own, 2), (rows, 1), 0, top)
    return jnp.take_along_axis(listing, (jnp.arange(top)[None, :] + rotation) % top, axis=1)


def shares(number_of, total, most, slope, full):
    loads = [(1 << 20) // math.isqrt(grade ** slope) + 1 for grade in range(1, number_of + 1)]
    largest = most if full else min(most, max(-(-total // number_of), total * loads[0] // sum(loads)))
    least = 1 if total - largest >= number_of - 1 else 0
    given, rest = [largest] + [least] * (number_of - 1), total - largest - least * (number_of - 1)
    while rest > 0:
        candidates = [i for i in range(1, number_of) if given[i] < largest] or [i for i in range(1, number_of) if given[i] < most]
        whole, budget = sum([loads[i] for i in candidates]), rest
        for i in candidates:
            extra = min(most - given[i], max(1, budget * loads[i] // whole), rest)
            given[i] = given[i] + extra
            rest = rest - extra
    return np.array(given)


def bell_draw(own_key, extent, spread, limit, split=(), kind=jnp.bfloat16):
    level = level_of(own_key, extent, split, -0.22, 0.18) if split else 1.0
    array = jax.random.normal(own_key, extent, jnp.float32) * spread * level
    return jnp.minimum(jnp.maximum(array, -limit), limit).astype(kind)


def setup_inputs(seed: int = 0) -> dict:
    splits = jax.random.split(jax.random.key(seed), 7)
    radiation = bell_draw(splits[0], (SLICES, GRID, 2, GRID), 1.0, 6.0, ((0, 256),), jnp.float32)
    phases = jnp.clip(jax.random.uniform(splits[1], (SLICES, NE), jnp.float32, -3.140625, 3.140625), -3.140625, 3.140625)
    energies = bell_draw(splits[2], (SLICES, NE), 1.0, 4.0, ((0, 256),), jnp.float32)
    cell_row = plant(jax.random.randint(splits[3], (SLICES, NE), 0, GRID), jax.random.fold_in(splits[3], 1), 0, GRID - 1).astype(jnp.int32)
    cell_col = plant(jax.random.randint(splits[4], (SLICES, NE), 0, GRID), jax.random.fold_in(splits[4], 1), 0, GRID - 1).astype(jnp.int32)
    landing_keys = jax.random.split(jax.random.fold_in(splits[5], 1), BLOCKS // BLK_DEV)
    landing_turns = jax.random.permutation(jax.random.fold_in(splits[5], 3), BLOCKS // BLK_DEV)
    landing = jax.vmap(lambda own, number: assign_block(jax.random.fold_in(splits[5], 2), own, number, BLK_DEV, N_SL, 1, MOST, 2))(landing_keys, landing_turns).reshape((BLOCKS, 1))
    return dict(radiation=radiation, phases=phases, energies=energies, cell_row=cell_row, cell_col=cell_col, landing=landing)


kick_gain = 0.3
phase_gain = 0.5
emit_gain = 1.0
chicane_r56 = 2.0


def propagator(grid_width):
    wave_index = jnp.arange(grid_width, dtype=jnp.int32)
    signed_wave = jnp.where(wave_index < grid_width - wave_index, wave_index, wave_index - grid_width).astype(jnp.float32)
    offset = jnp.minimum(wave_index, grid_width - wave_index)
    phase_turns = ((offset[:, None] * wave_index[None, :]) % grid_width).astype(jnp.float32)
    angles = phase_turns * (2.0 * math.pi / grid_width) - (4.0 * math.pi / (grid_width * grid_width)) * (signed_wave * signed_wave)[None, :]
    table_re = jnp.mean(jnp.cos(angles), axis=1)
    table_im = jnp.mean(jnp.sin(angles), axis=1)
    lag_index = ((wave_index[:, None] - wave_index[None, :]) % grid_width).astype(jnp.int32)
    return jnp.take(table_re, lag_index), jnp.take(table_im, lag_index)


def deposit(phases, targets, cell_row, cell_col):
    weight_re = lax.optimization_barrier(jnp.cos(phases).astype(jnp.bfloat16)).astype(jnp.float32)
    weight_im = lax.optimization_barrier((-jnp.sin(phases)).astype(jnp.bfloat16)).astype(jnp.float32)
    row_base = (targets.astype(jnp.int32) * GRID + cell_row.astype(jnp.int32)) * 2
    flat_re = (row_base * GRID + cell_col.astype(jnp.int32)).reshape(-1).astype(jnp.int32)
    flat_im = ((row_base + 1) * GRID + cell_col.astype(jnp.int32)).reshape(-1).astype(jnp.int32)
    grid_sum = jnp.zeros((SLICES * GRID * 2 * GRID,), jnp.float32)
    grid_sum = grid_sum.at[flat_re].add(weight_re.reshape(-1)).at[flat_im].add(weight_im.reshape(-1))
    return grid_sum.reshape(SLICES, GRID, 2, GRID)


def diffract(field_now, prop_real, prop_imag):
    exact_mode = lax.Precision.HIGHEST
    part_re = field_now[:, :, 0, :]
    part_im = field_now[:, :, 1, :]
    half_re = jnp.einsum('xz,szy->sxy', prop_real, part_re, precision=exact_mode) - jnp.einsum('xz,szy->sxy', prop_imag, part_im, precision=exact_mode)
    half_im = jnp.einsum('xz,szy->sxy', prop_real, part_im, precision=exact_mode) + jnp.einsum('xz,szy->sxy', prop_imag, part_re, precision=exact_mode)
    out_re = jnp.einsum('sxz,zy->sxy', half_re, prop_real, precision=exact_mode) - jnp.einsum('sxz,zy->sxy', half_im, prop_imag, precision=exact_mode)
    out_im = jnp.einsum('sxz,zy->sxy', half_re, prop_imag, precision=exact_mode) + jnp.einsum('sxz,zy->sxy', half_im, prop_real, precision=exact_mode)
    return jnp.stack([out_re, out_im], axis=2)


def reference(radiation, phases, energies, cell_row, cell_col, landing):
    cell_row = cell_row.astype(jnp.int32)
    cell_col = cell_col.astype(jnp.int32)
    landing = landing.astype(jnp.int32)
    prop_real, prop_imag = propagator(GRID)
    slice_ids = jnp.arange(SLICES, dtype=jnp.int32)[:, None]
    field_now = radiation
    for _ in range(STEPS):
        rounded = lax.optimization_barrier(field_now.astype(jnp.bfloat16))
        sample_re = rounded[slice_ids, cell_row, 0, cell_col].astype(jnp.float32)
        sample_im = rounded[slice_ids, cell_row, 1, cell_col].astype(jnp.float32)
        energies = energies + kick_gain * (sample_re * jnp.cos(phases) - sample_im * jnp.sin(phases))
        phases = phases + phase_gain * energies
        emitted = deposit(phases, slice_ids, cell_row, cell_col)
        field_now = field_now + emit_gain * emitted
        field_now = diffract(field_now, prop_real, prop_imag)
        field_now = jnp.concatenate([jnp.zeros_like(field_now[:1]), field_now[:-1]], axis=0)
    shifted = phases + chicane_r56 * energies
    per_slice = NE // EBLK
    block_ids = jnp.arange(BLOCKS, dtype=jnp.int32)
    source = block_ids // per_slice
    segment_span = S_DEV * N_SL
    destination = ((source // segment_span) * segment_span + landing[:, 0] * S_DEV + source % S_DEV).astype(jnp.int32)
    targets = jnp.repeat(destination, EBLK).reshape(SLICES, NE).astype(jnp.int32)
    bunching = deposit(shifted, targets, cell_row, cell_col)
    return field_now, bunching
```

```python
import functools
import math

import jax
import jax.numpy as jnp
import numpy as np
from jax import lax
from jax.experimental import pallas as pl
from jax.experimental.pallas import tpu as pltpu
from jax.sharding import PartitionSpec as P

GRID = 128
HALF = 64
NE = 4096
STEPS = 8
EBLK = 128
NBLK = NE // EBLK
BLK_DEV = 64
MOST = 4
CHUNK = 512

kick_gain = 0.3
phase_gain = 0.5
emit_gain = 1.0
chicane_r56 = 2.0

f32 = jnp.float32
bf16 = jnp.bfloat16
i32 = jnp.int32
MESH = pl.DeviceIdType.MESH


def propagator():
    k = np.arange(GRID)
    kf = np.where(k < GRID - k, k, k - GRID).astype(np.float64)
    o = np.minimum(k, GRID - k)
    turns = (o[:, None] * k[None, :] % GRID).astype(np.float64)
    angles = turns * (2.0 * math.pi / GRID) - 4.0 * math.pi / (GRID * GRID) * (kf * kf)[None, :]
    lag = (k[:, None] - k[None, :]) % GRID
    re = np.cos(angles).mean(axis=1).astype(np.float32)[lag]
    im = np.sin(angles).mean(axis=1).astype(np.float32)[lag]
    left = np.block([[re, -im], [im, re]]).astype(np.float32)
    high = left.astype(bf16)
    low = (left - high.astype(np.float32)).astype(bf16)
    return high, low


def split(x):
    high = x.astype(bf16)
    return high, (x - high.astype(f32)).astype(bf16)


def mm(a, b):
    return jnp.dot(a, b, preferred_element_type=f32)


def mm_nt(a, b):
    return lax.dot_general(a, b, (((1,), (1,)), ((), ())), preferred_element_type=f32)


def iota(shape, axis):
    return lax.broadcasted_iota(i32, shape, axis)


def kernel(
    comm,
    rad_ref, ph_ref, en_ref, row_ref, col_ref, land_ref, lhi_ref, llo_ref,
    rad_out, bun_out,
    hot, rhot, kidx, ridx, phs, ens, cs, sn, smp, spread,
    slots, cur, sent, left2, place,
    code_out, code_in, phase_out, phase_in,
    hot2, spread2, w2,
    slip_send, slip_recv, code_send, code_recv, phase_send, phase_recv,
):
    if comm:
        grp = lax.axis_index("grp")
        sl = lax.axis_index("sl")
        n_grp = lax.axis_size("grp")
        n_sl = lax.axis_size("sl")
        has_next = jnp.logical_or(sl < n_sl - 1, grp < n_grp - 1)
        has_prev = jnp.logical_or(sl > 0, grp > 0)
        next_sl = lax.rem(sl + 1, n_sl)
        next_grp = jnp.where(sl == n_sl - 1, jnp.minimum(grp + 1, n_grp - 1), grp)
        prev_sl = lax.rem(sl + n_sl - 1, n_sl)
        prev_grp = jnp.where(sl == 0, jnp.maximum(grp - 1, 0), grp)
        cross_next = jnp.logical_and(sl == n_sl - 1, grp < n_grp - 1)
        cross_prev = jnp.logical_and(sl == 0, grp > 0)
        barrier = pltpu.get_barrier_semaphore()

        @pl.loop(1, n_sl)
        def _(o):
            pl.semaphore_signal(
                barrier, inc=1, device_id=(grp, lax.rem(sl + o, n_sl)), device_id_type=MESH
            )

        @pl.when(cross_next)
        def _():
            pl.semaphore_signal(barrier, inc=1, device_id=(next_grp, next_sl), device_id_type=MESH)

        @pl.when(cross_prev)
        def _():
            pl.semaphore_signal(barrier, inc=1, device_id=(prev_grp, prev_sl), device_id_type=MESH)
    else:
        n_sl = 32

    for s in range(2):
        rows = row_ref[pl.ds(s, NBLK, stride=2), :]
        cols = col_ref[pl.ds(s, NBLK, stride=2), :]
        kidx[s] = (rows >> 6) * GRID + cols
        ridx[s] = rows & (HALF - 1)
        phs[s] = ph_ref[pl.ds(s, NBLK, stride=2), :]
        ens[s] = en_ref[pl.ds(s, NBLK, stride=2), :]
        cs[s] = jnp.cos(phs[s])
        sn[s] = jnp.sin(phs[s])
        for c in range(2):
            for h in range(2):
                piece = rad_ref[pl.ds(s * 256 + h * 128 + c, HALF, stride=2), :]
                if s == 0:
                    slots[0, 2 * c + h] = piece
                else:
                    cur[2 * c + h] = piece

        @pl.loop(0, NBLK)
        def _(j):
            lanes = pl.ds(pl.multiple_of(j * EBLK, EBLK), EBLK)
            kb = kidx[s, pl.ds(j, 1), :]
            rb = ridx[s, pl.ds(j, 1), :]
            hot[s, :, lanes] = (iota((256, EBLK), 0) == kb).astype(f32).astype(bf16)
            rhot[s, :, lanes] = (iota((HALF, EBLK), 0) == rb).astype(f32).astype(bf16)

    left2[0:256] = lhi_ref[...]
    left2[256:512] = llo_ref[...]

    land = jnp.broadcast_to(land_ref[...], (BLK_DEV, BLK_DEV))
    first, second = iota((BLK_DEV, BLK_DEV), 0), iota((BLK_DEV, BLK_DEV), 1)
    land_row = jnp.sum(jnp.where(first == second, land, 0), axis=0, keepdims=True)
    same = jnp.logical_and(land == land_row, first < second)
    earlier = jnp.sum(same.astype(i32), axis=0, keepdims=True)
    slot = land_row * MOST + earlier
    place[...] = (iota((2 * BLK_DEV, BLK_DEV), 0) == slot).astype(f32).astype(bf16)
    filled = jnp.sum(place[...].astype(f32), axis=1, keepdims=True)
    part = jnp.concatenate(
        [
            jnp.concatenate([ridx[0], ridx[1] + HALF], axis=0),
            jnp.concatenate([kidx[0], kidx[1]], axis=0),
        ],
        axis=1,
    ).astype(f32).astype(bf16)
    placed = mm(place[...], part)
    codes = (placed[:, :EBLK] + (filled - 1.0)) * 256.0 + placed[:, EBLK:]
    for p in range(32):
        code_out[p] = codes[p * MOST:(p + 1) * MOST]

    def exchange(out, inn, send, recv):
        if not comm:
            inn[...] = out[...]
            return
        inn[sl] = out[sl]

        @pl.loop(1, n_sl)
        def _(o):
            peer = lax.rem(sl + o, n_sl)
            pltpu.make_async_remote_copy(
                src_ref=out.at[peer], dst_ref=inn.at[sl], send_sem=send.at[o], recv_sem=recv.at[o],
                device_id=(grp, peer), device_id_type=MESH,
            ).start()

    def exchange_wait(out, inn, send, recv):
        if not comm:
            return

        @pl.loop(1, n_sl)
        def _(o):
            peer = lax.rem(sl + o, n_sl)
            source = lax.rem(sl + n_sl - o, n_sl)
            pltpu.make_async_remote_copy(
                src_ref=out.at[peer], dst_ref=inn.at[source], send_sem=send.at[o],
                recv_sem=recv.at[o], device_id=(grp, peer), device_id_type=MESH,
            ).wait()

    if comm:
        @pl.when(jnp.logical_not(has_prev))
        def _():
            @pl.loop(1, STEPS + 1)
            def _(t):
                slots[t] = jnp.zeros((4, HALF, GRID), f32)

        pl.semaphore_wait(
            barrier, n_sl - 1 + cross_next.astype(i32) + cross_prev.astype(i32)
        )
    exchange(code_out, code_in, code_send, code_recv)

    def kick(s, field):
        low = jnp.concatenate(
            [
                jnp.concatenate([field[0], field[1]], axis=1),
                jnp.concatenate([field[2], field[3]], axis=1),
            ],
            axis=0,
        ).astype(bf16)
        for j in range(NE // CHUNK):
            lanes = slice(j * CHUNK, (j + 1) * CHUNK)
            picked = mm(low, hot[s, :, lanes]).astype(bf16)
            pick = rhot[s, :, lanes]
            for c in range(2):
                prod = picked[c * HALF:(c + 1) * HALF] * pick
                quad = (prod[0:16] + prod[16:32]) + (prod[32:48] + prod[48:64])
                total = jnp.sum(quad.astype(f32), axis=0, keepdims=True)
                for b in range(CHUNK // EBLK):
                    row = j * (CHUNK // EBLK) + b
                    smp[c, row:row + 1, :] = total[:, b * EBLK:(b + 1) * EBLK]
        energy = ens[s] + kick_gain * (smp[0] * cs[s] - smp[1] * sn[s])
        phase = phs[s] + phase_gain * energy
        ens[s] = energy
        phs[s] = phase
        cs[s] = jnp.cos(phase)
        sn[s] = jnp.sin(phase)

    def emit(s, field):
        for j in range(NBLK):
            lanes = slice(j * EBLK, (j + 1) * EBLK)
            pick = rhot[s, :, lanes]
            spread[0:HALF, lanes] = pick * cs[s, j:j + 1, :].astype(bf16)
            spread[HALF:, lanes] = pick * (-sn[s, j:j + 1, :]).astype(bf16)
        emitted = mm_nt(spread[...], hot[s])
        full = jnp.concatenate(
            [
                field[2 * c + h] + emit_gain * emitted[c * HALF:(c + 1) * HALF, h * GRID:(h + 1) * GRID]
                for c in range(2)
                for h in range(2)
            ],
            axis=0,
        )
        high, low = split(full)
        q = mm(left2[...], jnp.concatenate([high, low], axis=1))
        half = (q[256:, GRID:] + (q[256:, :GRID] + q[:256, GRID:])) + q[:256, :GRID]
        wide = jnp.concatenate([half[:GRID], half[GRID:]], axis=1)
        high, low = split(wide)
        q = mm_nt(jnp.concatenate([high, low], axis=0), left2[0:256])
        out = (mm_nt(high, left2[256:512]) + q[GRID:]) + q[:GRID]
        return [out[h * HALF:(h + 1) * HALF, c * GRID:(c + 1) * GRID] for c in range(2) for h in range(2)]

    def slip_copy(t):
        return pltpu.make_async_remote_copy(
            src_ref=sent.at[t], dst_ref=slots.at[t + 1], send_sem=slip_send.at[t],
            recv_sem=slip_recv.at[t], device_id=(next_grp, next_sl), device_id_type=MESH,
        )

    def send_border(t, field):
        for i in range(4):
            sent[t, i] = field[i]
        if comm:
            @pl.when(has_next)
            def _():
                slip_copy(t).start()
        else:
            slots[t + 1] = sent[t]

    def wait_border(t):
        if comm:
            @pl.when(has_prev)
            def _():
                slip_copy(t).wait_recv()

    def load(ref):
        return [ref[i] for i in range(4)]

    @pl.loop(0, STEPS - 1)
    def _(t):
        kick(1, load(cur))
        send_border(t, emit(1, load(cur)))

        @pl.when(t > 0)
        def _():
            wait_border(t - 1)

        kick(0, load(slots.at[t]))
        moved = emit(0, load(slots.at[t]))
        for i in range(4):
            cur[i] = moved[i]

    last = STEPS - 1
    kick(1, load(cur))
    wait_border(last - 1)
    kick(0, load(slots.at[last]))
    final = jnp.concatenate([phs[s] + chicane_r56 * ens[s] for s in range(2)], axis=0)
    top = final.astype(bf16)
    rest = final - top.astype(f32)
    mid = rest.astype(bf16)
    tail = (rest - mid.astype(f32)).astype(bf16)
    placed = mm(place[...], jnp.concatenate([top, mid, tail], axis=1))
    out_phase = (placed[:, :EBLK] + placed[:, EBLK:2 * EBLK]) + placed[:, 2 * EBLK:]
    for p in range(32):
        phase_out[p] = out_phase[p * MOST:(p + 1) * MOST]
    exchange(phase_out, phase_in, phase_send, phase_recv)

    send_border(last, emit(1, load(cur)))
    moved = emit(0, load(slots.at[last]))
    for c in range(2):
        for h in range(2):
            rad_out[pl.ds(256 + h * 128 + c, HALF, stride=2), :] = moved[2 * c + h]

    exchange_wait(code_out, code_in, code_send, code_recv)

    @pl.loop(0, 32)
    def _(p):
        code = code_in[p].astype(i32)
        kb = code & 255
        rb = code >> 8
        for i in range(MOST):
            lanes = pl.ds(pl.multiple_of((p * MOST + i) * EBLK, EBLK), EBLK)
            hot2[:, lanes] = (iota((256, EBLK), 0) == kb[i:i + 1]).astype(f32).astype(bf16)
            spread2[0:GRID, lanes] = (iota((GRID, EBLK), 0) == rb[i:i + 1]).astype(f32).astype(bf16)

    exchange_wait(phase_out, phase_in, phase_send, phase_recv)

    @pl.loop(0, 32)
    def _(p):
        w2[0] = jnp.cos(phase_in[p])
        w2[1] = -jnp.sin(phase_in[p])
        for i in range(MOST):
            lanes = pl.ds(pl.multiple_of((p * MOST + i) * EBLK, EBLK), EBLK)
            pick = spread2[0:GRID, lanes]
            spread2[GRID:, lanes] = pick * w2[1, i:i + 1, :].astype(bf16)
            spread2[0:GRID, lanes] = pick * w2[0, i:i + 1, :].astype(bf16)

    landed = mm_nt(spread2[...], hot2[...])
    for c in range(2):
        for s in range(2):
            for h in range(2):
                bun_out[pl.ds(s * 256 + h * 128 + c, HALF, stride=2), :] = landed[
                    c * GRID + s * HALF:c * GRID + (s + 1) * HALF, h * GRID:(h + 1) * GRID
                ]

    wait_border(last)
    for c in range(2):
        for h in range(2):
            rad_out[pl.ds(h * 128 + c, HALF, stride=2), :] = slots[STEPS, 2 * c + h]
    if comm:
        @pl.when(has_next)
        def _():
            @pl.loop(0, STEPS)
            def _(t):
                slip_copy(t).wait_send()


def section(comm, rad, ph, en, row, col, land, lhi, llo):
    vmem = pl.BlockSpec(memory_space=pltpu.VMEM)
    field = (4, HALF, GRID)
    dense = (2, NBLK, EBLK)
    boxes = (32, MOST, EBLK)
    received = 32 * MOST * EBLK
    dma = pltpu.SemaphoreType.DMA
    return pl.pallas_call(
        functools.partial(kernel, comm),
        out_shape=(jax.ShapeDtypeStruct((512, GRID), f32), jax.ShapeDtypeStruct((512, GRID), f32)),
        in_specs=[vmem] * 8,
        out_specs=(vmem, vmem),
        scratch_shapes=[
            pltpu.VMEM((2, 256, NE), bf16),
            pltpu.VMEM((2, HALF, NE), bf16),
            pltpu.VMEM(dense, i32),
            pltpu.VMEM(dense, i32),
            pltpu.VMEM(dense, f32),
            pltpu.VMEM(dense, f32),
            pltpu.VMEM(dense, f32),
            pltpu.VMEM(dense, f32),
            pltpu.VMEM(dense, f32),
            pltpu.VMEM((2 * HALF, NE), bf16),
            pltpu.VMEM((STEPS + 1,) + field, f32),
            pltpu.VMEM(field, f32),
            pltpu.VMEM((STEPS,) + field, f32),
            pltpu.VMEM((512, 256), bf16),
            pltpu.VMEM((2 * BLK_DEV, BLK_DEV), bf16),
            pltpu.VMEM(boxes, f32),
            pltpu.VMEM(boxes, f32),
            pltpu.VMEM(boxes, f32),
            pltpu.VMEM(boxes, f32),
            pltpu.VMEM((256, received), bf16),
            pltpu.VMEM((256, received), bf16),
            pltpu.VMEM((2, MOST, EBLK), f32),
            dma((STEPS,)),
            dma((STEPS,)),
            dma((32,)),
            dma((32,)),
            dma((32,)),
            dma((32,)),
        ],
        compiler_params=pltpu.CompilerParams(
            collective_id=0 if comm else None, has_side_effects=comm, vmem_limit_bytes=56 << 20
        ),
    )(rad, ph, en, row, col, land, lhi, llo)


def dense_rows(x):
    return x.reshape(2, NBLK, EBLK).transpose(1, 0, 2).reshape(2 * NBLK, EBLK)


def shards(radiation, phases, energies, cell_row, cell_col, landing, comm=True):
    high, low = propagator()
    rad, bun = section(
        comm,
        radiation.reshape(512, GRID),
        dense_rows(phases),
        dense_rows(energies),
        dense_rows(cell_row),
        dense_rows(cell_col),
        landing,
        jnp.asarray(high),
        jnp.asarray(low),
    )
    return rad.reshape(2, GRID, 2, GRID), bun.reshape(2, GRID, 2, GRID)


def solution(mesh):
    both = ("grp", "sl")
    return jax.shard_map(
        shards,
        mesh=mesh,
        in_specs=(
            P(both, None, None, None),
            P(both, None),
            P(both, None),
            P(both, None),
            P(both, None),
            P(both, None),
        ),
        out_specs=(P(both, None, None, None), P(both, None, None, None)),
        check_vma=False,
    )
```

```python
import functools
import math

import jax
import jax.numpy as jnp
import numpy as np
from jax import lax
from jax.experimental import pallas as pl
from jax.experimental.pallas import tpu as pltpu
from jax.sharding import PartitionSpec as P

GRID = 128
HALF = 64
NE = 4096
STEPS = 8
EBLK = 128
NBLK = NE // EBLK
BLK_DEV = 64
MOST = 4
CHUNK = 512

kick_gain = 0.3
phase_gain = 0.5
emit_gain = 1.0
chicane_r56 = 2.0

f32 = jnp.float32
bf16 = jnp.bfloat16
i32 = jnp.int32
MESH = pl.DeviceIdType.MESH


def propagator():
    k = np.arange(GRID)
    kf = np.where(k < GRID - k, k, k - GRID).astype(np.float64)
    o = np.minimum(k, GRID - k)
    turns = (o[:, None] * k[None, :] % GRID).astype(np.float64)
    angles = turns * (2.0 * math.pi / GRID) - 4.0 * math.pi / (GRID * GRID) * (kf * kf)[None, :]
    lag = (k[:, None] - k[None, :]) % GRID
    re = np.cos(angles).mean(axis=1).astype(np.float32)[lag]
    im = np.sin(angles).mean(axis=1).astype(np.float32)[lag]
    left = np.block([[re, -im], [im, re]]).astype(np.float32)
    high = left.astype(bf16)
    low = (left - high.astype(np.float32)).astype(bf16)
    return high, low, np.ascontiguousarray(high.T), np.ascontiguousarray(low.T)


def split(x):
    high = x.astype(bf16)
    return high, (x - high.astype(f32)).astype(bf16)


def mm(a, b):
    return jnp.dot(a, b, preferred_element_type=f32)


def iota(shape, axis):
    return lax.broadcasted_iota(i32, shape, axis)


def onehot(index, shape, axis):
    places = iota(shape, axis).astype(f32).astype(bf16)
    return jnp.where(places == index, jnp.ones(shape, bf16), jnp.zeros(shape, bf16))


def transposed_onehots(index, out, picked, start):
    turned = index.T
    for n, j in enumerate(picked):
        out[pl.ds(start + n * EBLK, EBLK), :] = onehot(
            turned[:, j:j + 1].astype(bf16), (EBLK, 256), 1
        )


def kernel(
    comm,
    rad_ref, ph_ref, en_ref, row_ref, col_ref, land_ref, lhi_ref, llo_ref, rhi_ref, rlo_ref,
    rad_out, bun_out,
    hot, hot_t, rhot, kidx, ridx, phs, ens, cs, sn, smp, spread,
    slots, cur, sent, left2, place,
    code_out, code_in, phase_out, phase_in,
    hot2_t, spread2,
    slip_send, slip_recv, code_send, code_recv, phase_send, phase_recv,
):
    if comm:
        grp = lax.axis_index("grp")
        sl = lax.axis_index("sl")
        n_grp = lax.axis_size("grp")
        n_sl = lax.axis_size("sl")
        has_next = jnp.logical_or(sl < n_sl - 1, grp < n_grp - 1)
        has_prev = jnp.logical_or(sl > 0, grp > 0)
        next_sl = lax.rem(sl + 1, n_sl)
        next_grp = jnp.where(sl == n_sl - 1, jnp.minimum(grp + 1, n_grp - 1), grp)
        prev_sl = lax.rem(sl + n_sl - 1, n_sl)
        prev_grp = jnp.where(sl == 0, jnp.maximum(grp - 1, 0), grp)
        cross_next = jnp.logical_and(sl == n_sl - 1, grp < n_grp - 1)
        cross_prev = jnp.logical_and(sl == 0, grp > 0)
        barrier = pltpu.get_barrier_semaphore()

        @pl.loop(1, n_sl)
        def _(o):
            pl.semaphore_signal(
                barrier, inc=1, device_id=(grp, lax.rem(sl + o, n_sl)), device_id_type=MESH
            )

        @pl.when(cross_next)
        def _():
            pl.semaphore_signal(barrier, inc=1, device_id=(next_grp, next_sl), device_id_type=MESH)

        @pl.when(cross_prev)
        def _():
            pl.semaphore_signal(barrier, inc=1, device_id=(prev_grp, prev_sl), device_id_type=MESH)
    else:
        n_sl = 32

    for s in range(2):
        rows = row_ref[pl.ds(s, NBLK, stride=2), :]
        cols = col_ref[pl.ds(s, NBLK, stride=2), :]
        kidx[s] = (rows >> 6) * GRID + cols
        ridx[s] = rows & (HALF - 1)
        phs[s] = ph_ref[pl.ds(s, NBLK, stride=2), :]
        ens[s] = en_ref[pl.ds(s, NBLK, stride=2), :]
        cs[s] = jnp.cos(phs[s])
        sn[s] = jnp.sin(phs[s])
        for c in range(2):
            for h in range(2):
                piece = rad_ref[pl.ds(s * 256 + h * 128 + c, HALF, stride=2), :]
                if s == 0:
                    slots[0, 2 * c + h] = piece
                else:
                    cur[2 * c + h] = piece

        @pl.loop(0, NBLK)
        def _(j):
            lanes = pl.ds(pl.multiple_of(j * EBLK, EBLK), EBLK)
            kb = kidx[s, pl.ds(j, 1), :].astype(f32).astype(bf16)
            rb = ridx[s, pl.ds(j, 1), :].astype(f32).astype(bf16)
            hot[s, :, lanes] = onehot(kb, (256, EBLK), 0)
            rhot[s, :, lanes] = onehot(rb, (HALF, EBLK), 0)

        transposed_onehots(kidx[s].astype(f32), hot_t.at[s], range(NBLK), 0)

    left2[0:256] = lhi_ref[...]
    left2[256:512] = llo_ref[...]

    both = 2 * BLK_DEV
    land_row = jnp.broadcast_to(
        jnp.concatenate([land_ref[...], land_ref[...]], axis=1), (both, both)
    )
    first, second = iota((both, both), 0), iota((both, both), 1)
    land_col = jnp.sum(jnp.where(first == second, land_row, 0), axis=1, keepdims=True)
    same = jnp.logical_and(land_col == land_row, first < (second & (BLK_DEV - 1)))
    same = jnp.logical_and(same, first < BLK_DEV)
    earlier = jnp.sum(same.astype(i32), axis=0, keepdims=True)
    slot = land_row[0:1] * MOST + earlier
    box, column = iota((2 * both, both), 0), iota((2 * both, both), 1)
    fits = slot == (box >> 3) * MOST + (box & (MOST - 1))
    fits = jnp.logical_and(fits, ((box >> 2) & 1) == (column >> 6))
    place[...] = fits.astype(f32).astype(bf16)
    cells = jnp.concatenate([kidx[0], kidx[1], ridx[0], ridx[1] + HALF], axis=0)
    code_out[...] = mm(place[...], cells.astype(f32).astype(bf16)).reshape(32, 8, EBLK)

    def box_copy(o, out, inn, send, recv):
        peer = lax.rem(sl + o, n_sl)
        return pltpu.make_async_remote_copy(
            src_ref=out.at[peer], dst_ref=inn.at[o], send_sem=send.at[o], recv_sem=recv.at[o],
            device_id=(grp, peer), device_id_type=MESH,
        )

    def exchange(out, inn, send, recv):
        if not comm:
            inn[...] = out[...]
            return

        @pl.loop(1, n_sl)
        def _(o):
            box_copy(o, out, inn, send, recv).start()

        inn[0] = out[sl]

    def exchange_wait(out, inn, send, recv):
        if not comm:
            return

        @pl.loop(1, n_sl)
        def _(o):
            box_copy(o, out, inn, send, recv).wait()

    if comm:
        @pl.when(jnp.logical_not(has_prev))
        def _():
            @pl.loop(1, STEPS + 1)
            def _(t):
                slots[t] = jnp.zeros((4, HALF, GRID), f32)

        pl.semaphore_wait(
            barrier, n_sl - 1 + cross_next.astype(i32) + cross_prev.astype(i32)
        )
    exchange(code_out, code_in, code_send, code_recv)

    def kick(s, field):
        low = jnp.concatenate(
            [
                jnp.concatenate([field[0], field[1]], axis=1),
                jnp.concatenate([field[2], field[3]], axis=1),
            ],
            axis=0,
        ).astype(bf16)
        for j in range(NE // CHUNK):
            lanes = slice(j * CHUNK, (j + 1) * CHUNK)
            picked = mm(low, hot[s, :, lanes]).astype(bf16)
            pick = rhot[s, :, lanes]
            for c in range(2):
                prod = picked[c * HALF:(c + 1) * HALF] * pick
                quad = (prod[0:16] + prod[16:32]) + (prod[32:48] + prod[48:64])
                total = jnp.sum(quad.astype(f32), axis=0, keepdims=True)
                for b in range(CHUNK // EBLK):
                    row = j * (CHUNK // EBLK) + b
                    smp[c, row:row + 1, :] = total[:, b * EBLK:(b + 1) * EBLK]
        energy = ens[s] + kick_gain * (smp[0] * cs[s] - smp[1] * sn[s])
        phase = phs[s] + phase_gain * energy
        ens[s] = energy
        phs[s] = phase
        cs[s] = jnp.cos(phase)
        sn[s] = jnp.sin(phase)

    def emit(s, field):
        for j in range(NBLK):
            lanes = slice(j * EBLK, (j + 1) * EBLK)
            pick = rhot[s, :, lanes]
            spread[0:HALF, lanes] = pick * cs[s, j:j + 1, :].astype(bf16)
            spread[HALF:, lanes] = pick * (-sn[s, j:j + 1, :]).astype(bf16)
        emitted = mm(spread[...], hot_t[s])
        full = jnp.concatenate(
            [
                field[2 * c + h] + emit_gain * emitted[c * HALF:(c + 1) * HALF, h * GRID:(h + 1) * GRID]
                for c in range(2)
                for h in range(2)
            ],
            axis=0,
        )
        high, low = split(full)
        q = mm(left2[...], jnp.concatenate([high, low], axis=1))
        half = (q[256:, GRID:] + (q[256:, :GRID] + q[:256, GRID:])) + q[:256, :GRID]
        wide = jnp.concatenate([half[:GRID], half[GRID:]], axis=1)
        high, low = split(wide)
        q = mm(jnp.concatenate([high, low], axis=0), rhi_ref[...])
        out = (mm(high, rlo_ref[...]) + q[GRID:]) + q[:GRID]
        return [out[h * HALF:(h + 1) * HALF, c * GRID:(c + 1) * GRID] for c in range(2) for h in range(2)]

    def slip_copy(t):
        return pltpu.make_async_remote_copy(
            src_ref=sent.at[t], dst_ref=slots.at[t + 1], send_sem=slip_send.at[t],
            recv_sem=slip_recv.at[t], device_id=(next_grp, next_sl), device_id_type=MESH,
        )

    def send_border(t, field):
        for i in range(4):
            sent[t, i] = field[i]
        if comm:
            @pl.when(has_next)
            def _():
                slip_copy(t).start()
        else:
            pltpu.make_async_copy(sent.at[t], slots.at[t + 1], slip_send.at[t]).start()

    def wait_border(t):
        if comm:
            @pl.when(has_prev)
            def _():
                slip_copy(t).wait_recv()
        else:
            pltpu.make_async_copy(sent.at[t], slots.at[t + 1], slip_send.at[t]).wait()

    def load(ref):
        return [ref[i] for i in range(4)]

    @pl.loop(0, STEPS - 1)
    def _(t):
        kick(1, load(cur))
        send_border(t, emit(1, load(cur)))

        @pl.when(t > 0)
        def _():
            wait_border(t - 1)

        kick(0, load(slots.at[t]))
        moved = emit(0, load(slots.at[t]))
        for i in range(4):
            cur[i] = moved[i]

    last = STEPS - 1
    kick(1, load(cur))
    wait_border(last - 1)
    kick(0, load(slots.at[last]))
    final = jnp.concatenate([phs[s] + chicane_r56 * ens[s] for s in range(2)], axis=0)
    weights = jnp.concatenate([jnp.cos(final), -jnp.sin(final)], axis=0).astype(bf16)
    phase_out[...] = mm(place[...], weights).reshape(32, 8, EBLK)
    exchange(phase_out, phase_in, phase_send, phase_recv)

    send_border(last, emit(1, load(cur)))
    moved = emit(0, load(slots.at[last]))
    for c in range(2):
        for h in range(2):
            rad_out[pl.ds(256 + h * 128 + c, HALF, stride=2), :] = moved[2 * c + h]

    exchange_wait(code_out, code_in, code_send, code_recv)

    for p in range(0, 32, 4):
        cells = jnp.concatenate([code_in[p + n] for n in range(4)], axis=0)
        picked = [8 * n + i for n in range(4) for i in range(MOST)]
        transposed_onehots(cells, hot2_t, picked, p * MOST * EBLK)

    exchange_wait(phase_out, phase_in, phase_send, phase_recv)

    @pl.loop(0, 32)
    def _(p):
        for i in range(MOST):
            lanes = pl.ds(pl.multiple_of((p * MOST + i) * EBLK, EBLK), EBLK)
            rb = code_in[p, MOST + i:MOST + i + 1, :].astype(bf16)
            here = iota((GRID, EBLK), 0).astype(f32).astype(bf16) == rb
            for c in range(2):
                w = phase_in[p, c * MOST + i:c * MOST + i + 1, :].astype(bf16)
                w = jnp.broadcast_to(w, (GRID, EBLK))
                spread2[c * GRID:(c + 1) * GRID, lanes] = jnp.where(here, w, jnp.zeros_like(w))

    landed = mm(spread2[...], hot2_t[...])
    for c in range(2):
        for s in range(2):
            for h in range(2):
                bun_out[pl.ds(s * 256 + h * 128 + c, HALF, stride=2), :] = landed[
                    c * GRID + s * HALF:c * GRID + (s + 1) * HALF, h * GRID:(h + 1) * GRID
                ]

    wait_border(last)
    for c in range(2):
        for h in range(2):
            rad_out[pl.ds(h * 128 + c, HALF, stride=2), :] = slots[STEPS, 2 * c + h]
    if comm:
        @pl.when(has_next)
        def _():
            @pl.loop(0, STEPS)
            def _(t):
                slip_copy(t).wait_send()


def section(comm, *args):
    vmem = pl.BlockSpec(memory_space=pltpu.VMEM)
    field = (4, HALF, GRID)
    dense = (2, NBLK, EBLK)
    boxes = (32, 2 * MOST, EBLK)
    received = 32 * MOST * EBLK
    dma = pltpu.SemaphoreType.DMA
    return pl.pallas_call(
        functools.partial(kernel, comm),
        out_shape=(jax.ShapeDtypeStruct((512, GRID), f32), jax.ShapeDtypeStruct((512, GRID), f32)),
        in_specs=[vmem] * 10,
        out_specs=(vmem, vmem),
        scratch_shapes=[
            pltpu.VMEM((2, 256, NE), bf16),
            pltpu.VMEM((2, NE, 256), bf16),
            pltpu.VMEM((2, HALF, NE), bf16),
            pltpu.VMEM(dense, i32),
            pltpu.VMEM(dense, i32),
            pltpu.VMEM(dense, f32),
            pltpu.VMEM(dense, f32),
            pltpu.VMEM(dense, f32),
            pltpu.VMEM(dense, f32),
            pltpu.VMEM(dense, f32),
            pltpu.VMEM((2 * HALF, NE), bf16),
            pltpu.VMEM((STEPS + 1,) + field, f32),
            pltpu.VMEM(field, f32),
            pltpu.VMEM((STEPS,) + field, f32),
            pltpu.VMEM((512, 256), bf16),
            pltpu.VMEM((4 * BLK_DEV, 2 * BLK_DEV), bf16),
            pltpu.VMEM(boxes, f32),
            pltpu.VMEM(boxes, f32),
            pltpu.VMEM(boxes, f32),
            pltpu.VMEM(boxes, f32),
            pltpu.VMEM((received, 256), bf16),
            pltpu.VMEM((256, received), bf16),
            dma((STEPS,)),
            dma((STEPS,)),
            dma((32,)),
            dma((32,)),
            dma((32,)),
            dma((32,)),
        ],
        compiler_params=pltpu.CompilerParams(
            collective_id=0 if comm else None, has_side_effects=comm, vmem_limit_bytes=56 << 20
        ),
    )(*args)


def dense_rows(x):
    return x.reshape(2, NBLK, EBLK).transpose(1, 0, 2).reshape(2 * NBLK, EBLK)


def shards(radiation, phases, energies, cell_row, cell_col, landing, comm=True):
    rad, bun = section(
        comm,
        radiation.reshape(512, GRID),
        dense_rows(phases),
        dense_rows(energies),
        dense_rows(cell_row),
        dense_rows(cell_col),
        landing.reshape(1, BLK_DEV),
        *[jnp.asarray(part) for part in propagator()],
    )
    return rad.reshape(2, GRID, 2, GRID), bun.reshape(2, GRID, 2, GRID)


def solution(mesh):
    both = ("grp", "sl")
    return jax.shard_map(
        shards,
        mesh=mesh,
        in_specs=(
            P(both, None, None, None),
            P(both, None),
            P(both, None),
            P(both, None),
            P(both, None),
            P(both, None),
        ),
        out_specs=(P(both, None, None, None), P(both, None, None, None)),
        check_vma=False,
    )
```

```python
import functools
import math

import jax
import jax.numpy as jnp
import numpy as np
from jax import lax
from jax.experimental import pallas as pl
from jax.experimental.pallas import tpu as pltpu
from jax.sharding import PartitionSpec as P

GRID = 128
HALF = 64
NE = 4096
STEPS = 8
EBLK = 128
NBLK = NE // EBLK
BLK_DEV = 64
MOST = 4
CHUNK = 512

kick_gain = 0.3
phase_gain = 0.5
emit_gain = 1.0
chicane_r56 = 2.0

f32 = jnp.float32
bf16 = jnp.bfloat16
i32 = jnp.int32
MESH = pl.DeviceIdType.MESH


def propagator():
    k = np.arange(GRID)
    kf = np.where(k < GRID - k, k, k - GRID).astype(np.float64)
    o = np.minimum(k, GRID - k)
    turns = (o[:, None] * k[None, :] % GRID).astype(np.float64)
    angles = turns * (2.0 * math.pi / GRID) - 4.0 * math.pi / (GRID * GRID) * (kf * kf)[None, :]
    lag = (k[:, None] - k[None, :]) % GRID
    re = np.cos(angles).mean(axis=1).astype(np.float32)[lag]
    im = np.sin(angles).mean(axis=1).astype(np.float32)[lag]
    left = np.block([[re, -im], [im, re]]).astype(np.float32)
    high = left.astype(bf16)
    low = (left - high.astype(np.float32)).astype(bf16)
    return high, low, np.ascontiguousarray(high.T), np.ascontiguousarray(low.T)


def split(x):
    high = x.astype(bf16)
    return high, (x - high.astype(f32)).astype(bf16)


def mm(a, b):
    return jnp.dot(a, b, preferred_element_type=f32)


def iota(shape, axis):
    return lax.broadcasted_iota(i32, shape, axis)


def onehot(index, shape, axis):
    places = iota(shape, axis).astype(f32).astype(bf16)
    return jnp.where(places == index, jnp.ones(shape, bf16), jnp.zeros(shape, bf16))


def transposed_onehots(index, out, picked, start):
    turned = index.T
    for n, j in enumerate(picked):
        out[pl.ds(start + n * EBLK, EBLK), :] = onehot(
            turned[:, j:j + 1].astype(bf16), (EBLK, 256), 1
        )


def kernel(
    comm,
    rad_ref, ph_ref, en_ref, row_ref, col_ref, land_ref, lhi_ref, llo_ref, rhi_ref, rlo_ref,
    rad_out, bun_out,
    hot, hot_t, rhot, kidx, ridx, phs, ens, cs, sn, smp, spread,
    slots, cur, sent, place,
    code_out, code_in, phase_out, phase_in,
    hot2_t, spread2,
    slip_send, slip_recv, code_send, code_recv, phase_send, phase_recv,
):
    if comm:
        grp = lax.axis_index("grp")
        sl = lax.axis_index("sl")
        n_grp = lax.axis_size("grp")
        n_sl = lax.axis_size("sl")
        has_next = jnp.logical_or(sl < n_sl - 1, grp < n_grp - 1)
        has_prev = jnp.logical_or(sl > 0, grp > 0)
        next_sl = lax.rem(sl + 1, n_sl)
        next_grp = jnp.where(sl == n_sl - 1, jnp.minimum(grp + 1, n_grp - 1), grp)
        prev_sl = lax.rem(sl + n_sl - 1, n_sl)
        prev_grp = jnp.where(sl == 0, jnp.maximum(grp - 1, 0), grp)
        cross_next = jnp.logical_and(sl == n_sl - 1, grp < n_grp - 1)
        cross_prev = jnp.logical_and(sl == 0, grp > 0)
        barrier = pltpu.get_barrier_semaphore()

        for o in range(1, n_sl):
            pl.semaphore_signal(
                barrier, inc=1, device_id=(grp, lax.rem(sl + o, n_sl)), device_id_type=MESH
            )

        @pl.when(cross_next)
        def _():
            pl.semaphore_signal(barrier, inc=1, device_id=(next_grp, next_sl), device_id_type=MESH)

        @pl.when(cross_prev)
        def _():
            pl.semaphore_signal(barrier, inc=1, device_id=(prev_grp, prev_sl), device_id_type=MESH)
    else:
        n_sl = 32

    for s in range(2):
        rows = row_ref[pl.ds(s, NBLK, stride=2), :]
        cols = col_ref[pl.ds(s, NBLK, stride=2), :]
        kidx[s] = (rows >> 6) * GRID + cols
        ridx[s] = rows & (HALF - 1)
        phs[s] = ph_ref[pl.ds(s, NBLK, stride=2), :]
        ens[s] = en_ref[pl.ds(s, NBLK, stride=2), :]
        cs[s] = jnp.cos(phs[s])
        sn[s] = jnp.sin(phs[s])
        for c in range(2):
            for h in range(2):
                piece = rad_ref[pl.ds(s * 256 + h * 128 + c, HALF, stride=2), :]
                if s == 0:
                    slots[0, 2 * c + h] = piece
                else:
                    cur[2 * c + h] = piece

        for j in range(NBLK):
            lanes = slice(j * EBLK, (j + 1) * EBLK)
            kb = kidx[s, j:j + 1, :].astype(f32).astype(bf16)
            rb = ridx[s, j:j + 1, :].astype(f32).astype(bf16)
            hot[s, :, lanes] = onehot(kb, (256, EBLK), 0)
            rhot[s, :, lanes] = onehot(rb, (HALF, EBLK), 0)

        transposed_onehots(kidx[s].astype(f32), hot_t.at[s], range(NBLK), 0)

    both = 2 * BLK_DEV
    land_row = jnp.broadcast_to(
        jnp.concatenate([land_ref[...], land_ref[...]], axis=1), (both, both)
    )
    first, second = iota((both, both), 0), iota((both, both), 1)
    land_col = jnp.sum(jnp.where(first == second, land_row, 0), axis=1, keepdims=True)
    same = jnp.logical_and(land_col == land_row, first < (second & (BLK_DEV - 1)))
    same = jnp.logical_and(same, first < BLK_DEV)
    earlier = jnp.sum(same.astype(i32), axis=0, keepdims=True)
    slot = land_row[0:1] * MOST + earlier
    box, column = iota((2 * both, both), 0), iota((2 * both, both), 1)
    fits = slot == (box >> 3) * MOST + (box & (MOST - 1))
    fits = jnp.logical_and(fits, ((box >> 2) & 1) == (column >> 6))
    place[...] = fits.astype(f32).astype(bf16)
    cells = jnp.concatenate([kidx[0], kidx[1], ridx[0], ridx[1] + HALF], axis=0)
    code_out[...] = mm(place[...], cells.astype(f32).astype(bf16)).reshape(32, 8, EBLK)

    def box_copy(o, out, inn, send, recv):
        peer = lax.rem(sl + o, n_sl)
        return pltpu.make_async_remote_copy(
            src_ref=out.at[peer], dst_ref=inn.at[o], send_sem=send.at[0], recv_sem=recv.at[0],
            device_id=(grp, peer), device_id_type=MESH,
        )

    def exchange(out, inn, send, recv):
        if not comm:
            inn[...] = out[...]
            return

        for o in range(1, n_sl):
            box_copy(o, out, inn, send, recv).start()

        inn[0] = out[sl]

    def exchange_wait(out, inn, send, recv):
        if not comm:
            return

        boxes = pltpu.make_async_remote_copy(
            src_ref=out.at[pl.ds(1, n_sl - 1)], dst_ref=inn.at[pl.ds(1, n_sl - 1)],
            send_sem=send.at[0], recv_sem=recv.at[0],
            device_id=(grp, lax.rem(sl + 1, n_sl)), device_id_type=MESH,
        )
        boxes.wait_recv()
        boxes.wait_send()

    if comm:
        @pl.when(jnp.logical_not(has_prev))
        def _():
            @pl.loop(1, STEPS + 1)
            def _(t):
                slots[t] = jnp.zeros((4, HALF, GRID), f32)

        pl.semaphore_wait(
            barrier, n_sl - 1 + cross_next.astype(i32) + cross_prev.astype(i32)
        )
    exchange(code_out, code_in, code_send, code_recv)

    def kick(s, field):
        low = jnp.concatenate(
            [
                jnp.concatenate([field[0], field[1]], axis=1),
                jnp.concatenate([field[2], field[3]], axis=1),
            ],
            axis=0,
        ).astype(bf16)
        for j in range(NE // CHUNK):
            lanes = slice(j * CHUNK, (j + 1) * CHUNK)
            picked = mm(low, hot[s, :, lanes]).astype(bf16)
            pick = rhot[s, :, lanes]
            for c in range(2):
                prod = picked[c * HALF:(c + 1) * HALF] * pick
                quad = (prod[0:16] + prod[16:32]) + (prod[32:48] + prod[48:64])
                total = jnp.sum(quad.astype(f32), axis=0, keepdims=True)
                for b in range(CHUNK // EBLK):
                    row = j * (CHUNK // EBLK) + b
                    smp[c, row:row + 1, :] = total[:, b * EBLK:(b + 1) * EBLK]
        energy = ens[s] + kick_gain * (smp[0] * cs[s] - smp[1] * sn[s])
        phase = phs[s] + phase_gain * energy
        ens[s] = energy
        phs[s] = phase
        cs[s] = jnp.cos(phase)
        sn[s] = jnp.sin(phase)

    def emit(s, field):
        for j in range(NBLK):
            lanes = slice(j * EBLK, (j + 1) * EBLK)
            pick = rhot[s, :, lanes]
            spread[0:HALF, lanes] = pick * cs[s, j:j + 1, :].astype(bf16)
            spread[HALF:, lanes] = pick * (-sn[s, j:j + 1, :]).astype(bf16)
        emitted = mm(spread[...], hot_t[s])
        full = jnp.concatenate(
            [
                field[2 * c + h] + emit_gain * emitted[c * HALF:(c + 1) * HALF, h * GRID:(h + 1) * GRID]
                for c in range(2)
                for h in range(2)
            ],
            axis=0,
        )
        high, low = split(full)
        both = jnp.concatenate([high, low], axis=1)
        outs = []
        for h in range(2):
            first = slice(h * HALF, (h + 1) * HALF)
            second = slice(GRID + h * HALF, GRID + (h + 1) * HALF)
            left_hi = jnp.concatenate([lhi_ref[first], lhi_ref[second]], axis=0)
            left_lo = jnp.concatenate([llo_ref[first], llo_ref[second]], axis=0)
            q = mm(left_hi, both)
            half = (mm(left_lo, high) + q[:, GRID:]) + q[:, :GRID]
            wide_hi, wide_lo = split(jnp.concatenate([half[:HALF], half[HALF:]], axis=1))
            q = mm(jnp.concatenate([wide_hi, wide_lo], axis=0), rhi_ref[...])
            outs.append((mm(wide_hi, rlo_ref[...]) + q[HALF:]) + q[:HALF])
        return [outs[h][:, c * GRID:(c + 1) * GRID] for c in range(2) for h in range(2)]

    def slip_copy(t):
        return pltpu.make_async_remote_copy(
            src_ref=sent.at[t], dst_ref=slots.at[t + 1], send_sem=slip_send.at[t],
            recv_sem=slip_recv.at[t], device_id=(next_grp, next_sl), device_id_type=MESH,
        )

    def send_border(t, field):
        for i in range(4):
            sent[t, i] = field[i]
        if comm:
            @pl.when(has_next)
            def _():
                slip_copy(t).start()
        else:
            pltpu.make_async_copy(sent.at[t], slots.at[t + 1], slip_send.at[t]).start()

    def wait_border(t):
        if comm:
            @pl.when(has_prev)
            def _():
                slip_copy(t).wait_recv()
        else:
            pltpu.make_async_copy(sent.at[t], slots.at[t + 1], slip_send.at[t]).wait()

    def load(ref):
        return [ref[i] for i in range(4)]

    @pl.loop(0, STEPS - 1)
    def _(t):
        kick(1, load(cur))
        send_border(t, emit(1, load(cur)))

        @pl.when(t > 0)
        def _():
            wait_border(t - 1)

        kick(0, load(slots.at[t]))
        moved = emit(0, load(slots.at[t]))
        for i in range(4):
            cur[i] = moved[i]

    last = STEPS - 1
    kick(1, load(cur))
    wait_border(last - 1)
    kick(0, load(slots.at[last]))
    final = jnp.concatenate([phs[s] + chicane_r56 * ens[s] for s in range(2)], axis=0)
    weights = jnp.concatenate([jnp.cos(final), -jnp.sin(final)], axis=0).astype(bf16)
    phase_out[...] = mm(place[...], weights).reshape(32, 8, EBLK)
    exchange(phase_out, phase_in, phase_send, phase_recv)

    send_border(last, emit(1, load(cur)))
    moved = emit(0, load(slots.at[last]))
    for c in range(2):
        for h in range(2):
            rad_out[pl.ds(256 + h * 128 + c, HALF, stride=2), :] = moved[2 * c + h]

    exchange_wait(code_out, code_in, code_send, code_recv)

    for p in range(0, 32, 4):
        cells = jnp.concatenate([code_in[p + n] for n in range(4)], axis=0)
        picked = [8 * n + i for n in range(4) for i in range(MOST)]
        transposed_onehots(cells, hot2_t, picked, p * MOST * EBLK)

    exchange_wait(phase_out, phase_in, phase_send, phase_recv)

    for p in range(32):
        for i in range(MOST):
            lanes = slice((p * MOST + i) * EBLK, (p * MOST + i + 1) * EBLK)
            rb = code_in[p, MOST + i:MOST + i + 1, :].astype(bf16)
            here = iota((GRID, EBLK), 0).astype(f32).astype(bf16) == rb
            for c in range(2):
                w = phase_in[p, c * MOST + i:c * MOST + i + 1, :].astype(bf16)
                w = jnp.broadcast_to(w, (GRID, EBLK))
                spread2[c * GRID:(c + 1) * GRID, lanes] = jnp.where(here, w, jnp.zeros_like(w))

    landed = mm(spread2[...], hot2_t[...])
    for c in range(2):
        for s in range(2):
            for h in range(2):
                bun_out[pl.ds(s * 256 + h * 128 + c, HALF, stride=2), :] = landed[
                    c * GRID + s * HALF:c * GRID + (s + 1) * HALF, h * GRID:(h + 1) * GRID
                ]

    wait_border(last)
    for c in range(2):
        for h in range(2):
            rad_out[pl.ds(h * 128 + c, HALF, stride=2), :] = slots[STEPS, 2 * c + h]
    if comm:
        @pl.when(has_next)
        def _():
            @pl.loop(0, STEPS)
            def _(t):
                slip_copy(t).wait_send()


def section(comm, *args):
    vmem = pl.BlockSpec(memory_space=pltpu.VMEM)
    field = (4, HALF, GRID)
    dense = (2, NBLK, EBLK)
    boxes = (32, 2 * MOST, EBLK)
    received = 32 * MOST * EBLK
    dma = pltpu.SemaphoreType.DMA
    return pl.pallas_call(
        functools.partial(kernel, comm),
        out_shape=(jax.ShapeDtypeStruct((512, GRID), f32), jax.ShapeDtypeStruct((512, GRID), f32)),
        in_specs=[vmem] * 10,
        out_specs=(vmem, vmem),
        scratch_shapes=[
            pltpu.VMEM((2, 256, NE), bf16),
            pltpu.VMEM((2, NE, 256), bf16),
            pltpu.VMEM((2, HALF, NE), bf16),
            pltpu.VMEM(dense, i32),
            pltpu.VMEM(dense, i32),
            pltpu.VMEM(dense, f32),
            pltpu.VMEM(dense, f32),
            pltpu.VMEM(dense, f32),
            pltpu.VMEM(dense, f32),
            pltpu.VMEM(dense, f32),
            pltpu.VMEM((2 * HALF, NE), bf16),
            pltpu.VMEM((STEPS + 1,) + field, f32),
            pltpu.VMEM(field, f32),
            pltpu.VMEM((STEPS,) + field, f32),
            pltpu.VMEM((4 * BLK_DEV, 2 * BLK_DEV), bf16),
            pltpu.VMEM(boxes, f32),
            pltpu.VMEM(boxes, f32),
            pltpu.VMEM(boxes, f32),
            pltpu.VMEM(boxes, f32),
            pltpu.VMEM((received, 256), bf16),
            pltpu.VMEM((256, received), bf16),
            dma((STEPS,)),
            dma((STEPS,)),
            dma((1,)),
            dma((1,)),
            dma((1,)),
            dma((1,)),
        ],
        compiler_params=pltpu.CompilerParams(
            collective_id=0 if comm else None, has_side_effects=comm, vmem_limit_bytes=56 << 20
        ),
    )(*args)


def dense_rows(x):
    return x.reshape(2, NBLK, EBLK).transpose(1, 0, 2).reshape(2 * NBLK, EBLK)


def shards(radiation, phases, energies, cell_row, cell_col, landing, comm=True):
    rad, bun = section(
        comm,
        radiation.reshape(512, GRID),
        dense_rows(phases),
        dense_rows(energies),
        dense_rows(cell_row),
        dense_rows(cell_col),
        landing.reshape(1, BLK_DEV),
        *[jnp.asarray(part) for part in propagator()],
    )
    return rad.reshape(2, GRID, 2, GRID), bun.reshape(2, GRID, 2, GRID)


def solution(mesh):
    both = ("grp", "sl")
    return jax.shard_map(
        shards,
        mesh=mesh,
        in_specs=(
            P(both, None, None, None),
            P(both, None),
            P(both, None),
            P(both, None),
            P(both, None),
            P(both, None),
        ),
        out_specs=(P(both, None, None, None), P(both, None, None, None)),
        check_vma=False,
    )
```

```python
import functools
import math

import jax
import jax.numpy as jnp
import numpy as np
from jax import lax
from jax.experimental import pallas as pl
from jax.experimental.pallas import tpu as pltpu
from jax.sharding import PartitionSpec as P

GRID = 128
HALF = 64
NE = 4096
STEPS = 8
EBLK = 128
NBLK = NE // EBLK
BLK_DEV = 64
MOST = 4
CHUNK = 512

kick_gain = 0.3
phase_gain = 0.5
emit_gain = 1.0
chicane_r56 = 2.0

f32 = jnp.float32
bf16 = jnp.bfloat16
i32 = jnp.int32
MESH = pl.DeviceIdType.MESH


def propagator():
    k = np.arange(GRID)
    kf = np.where(k < GRID - k, k, k - GRID).astype(np.float64)
    o = np.minimum(k, GRID - k)
    turns = (o[:, None] * k[None, :] % GRID).astype(np.float64)
    angles = turns * (2.0 * math.pi / GRID) - 4.0 * math.pi / (GRID * GRID) * (kf * kf)[None, :]
    lag = (k[:, None] - k[None, :]) % GRID
    re = np.cos(angles).mean(axis=1).astype(np.float32)[lag]
    im = np.sin(angles).mean(axis=1).astype(np.float32)[lag]
    left = np.block([[re, -im], [im, re]]).astype(np.float32)
    high = left.astype(bf16)
    low = (left - high.astype(np.float32)).astype(bf16)
    return high, low, np.ascontiguousarray(high.T), np.ascontiguousarray(low.T)


def split(x):
    high = x.astype(bf16)
    return high, (x - high.astype(f32)).astype(bf16)


def mm(a, b):
    return jnp.dot(a, b, preferred_element_type=f32)


def iota(shape, axis):
    return lax.broadcasted_iota(i32, shape, axis)


def onehot(index, shape, axis):
    places = iota(shape, axis).astype(f32).astype(bf16)
    return jnp.where(places == index, jnp.ones(shape, bf16), jnp.zeros(shape, bf16))


def transposed_onehots(index, out, picked, start):
    turned = index.T
    for n, j in enumerate(picked):
        out[pl.ds(start + n * EBLK, EBLK), :] = onehot(
            turned[:, j:j + 1].astype(bf16), (EBLK, 256), 1
        )


def kernel(
    comm,
    rad_in, ph_in, en_in, row_in, col_in, land_in, lhi_in, llo_in, rhi_in, rlo_in,
    rad_out, bun_out,
    rad_ref, ph_ref, en_ref, row_ref, col_ref, land_ref, lhi_ref, llo_ref, rhi_ref, rlo_ref, in_sem,
    hot, hot_t, rhot, kidx, ridx, phs, ens, cs, sn, smp, spread,
    slots, cur, sent, place,
    code_out, code_in, phase_out, phase_in,
    hot2_t, spread2,
    slip_send, slip_recv, code_send, code_recv, phase_send, phase_recv,
):
    loads = [
        pltpu.make_async_copy(source, target, in_sem.at[n])
        for n, (source, target) in enumerate([
            (row_in, row_ref), (col_in, col_ref), (ph_in, ph_ref), (en_in, en_ref),
            (rad_in, rad_ref), (land_in, land_ref), (lhi_in, lhi_ref), (llo_in, llo_ref),
            (rhi_in, rhi_ref), (rlo_in, rlo_ref),
        ])
    ]
    for one in loads:
        one.start()
    if comm:
        grp = lax.axis_index("grp")
        sl = lax.axis_index("sl")
        n_grp = lax.axis_size("grp")
        n_sl = lax.axis_size("sl")
        has_next = jnp.logical_or(sl < n_sl - 1, grp < n_grp - 1)
        has_prev = jnp.logical_or(sl > 0, grp > 0)
        next_sl = lax.rem(sl + 1, n_sl)
        next_grp = jnp.where(sl == n_sl - 1, jnp.minimum(grp + 1, n_grp - 1), grp)
        prev_sl = lax.rem(sl + n_sl - 1, n_sl)
        prev_grp = jnp.where(sl == 0, jnp.maximum(grp - 1, 0), grp)
        cross_next = jnp.logical_and(sl == n_sl - 1, grp < n_grp - 1)
        cross_prev = jnp.logical_and(sl == 0, grp > 0)
        barrier = pltpu.get_barrier_semaphore()

        for o in range(1, n_sl):
            pl.semaphore_signal(
                barrier, inc=1, device_id=(grp, lax.rem(sl + o, n_sl)), device_id_type=MESH
            )

        @pl.when(cross_next)
        def _():
            pl.semaphore_signal(barrier, inc=1, device_id=(next_grp, next_sl), device_id_type=MESH)

        @pl.when(cross_prev)
        def _():
            pl.semaphore_signal(barrier, inc=1, device_id=(prev_grp, prev_sl), device_id_type=MESH)
    else:
        n_sl = 32

    for one in loads[:2]:
        one.wait()
    for s in range(2):
        rows = row_ref[pl.ds(s, NBLK, stride=2), :]
        cols = col_ref[pl.ds(s, NBLK, stride=2), :]
        kidx[s] = (rows >> 6) * GRID + cols
        ridx[s] = rows & (HALF - 1)
        for j in range(NBLK):
            lanes = slice(j * EBLK, (j + 1) * EBLK)
            kb = kidx[s, j:j + 1, :].astype(f32).astype(bf16)
            rb = ridx[s, j:j + 1, :].astype(f32).astype(bf16)
            hot[s, :, lanes] = onehot(kb, (256, EBLK), 0)
            rhot[s, :, lanes] = onehot(rb, (HALF, EBLK), 0)

        transposed_onehots(kidx[s].astype(f32), hot_t.at[s], range(NBLK), 0)

    for one in loads[2:]:
        one.wait()
    for s in range(2):
        phs[s] = ph_ref[pl.ds(s, NBLK, stride=2), :]
        ens[s] = en_ref[pl.ds(s, NBLK, stride=2), :]
        cs[s] = jnp.cos(phs[s])
        sn[s] = jnp.sin(phs[s])
        for c in range(2):
            for h in range(2):
                piece = rad_ref[pl.ds(s * 256 + h * 128 + c, HALF, stride=2), :]
                if s == 0:
                    slots[0, 2 * c + h] = piece
                else:
                    cur[2 * c + h] = piece

    both = 2 * BLK_DEV
    land_row = jnp.broadcast_to(
        jnp.concatenate([land_ref[...], land_ref[...]], axis=1), (both, both)
    )
    first, second = iota((both, both), 0), iota((both, both), 1)
    land_col = jnp.sum(jnp.where(first == second, land_row, 0), axis=1, keepdims=True)
    same = jnp.logical_and(land_col == land_row, first < (second & (BLK_DEV - 1)))
    same = jnp.logical_and(same, first < BLK_DEV)
    earlier = jnp.sum(same.astype(i32), axis=0, keepdims=True)
    slot = land_row[0:1] * MOST + earlier
    box, column = iota((2 * both, both), 0), iota((2 * both, both), 1)
    fits = slot == (box >> 3) * MOST + (box & (MOST - 1))
    fits = jnp.logical_and(fits, ((box >> 2) & 1) == (column >> 6))
    place[...] = fits.astype(f32).astype(bf16)
    cells = jnp.concatenate([kidx[0], kidx[1], ridx[0], ridx[1] + HALF], axis=0)
    code_out[...] = mm(place[...], cells.astype(f32).astype(bf16)).reshape(32, 8, EBLK)

    def box_copy(o, out, inn, send, recv):
        peer = lax.rem(sl + o, n_sl)
        return pltpu.make_async_remote_copy(
            src_ref=out.at[peer], dst_ref=inn.at[o], send_sem=send.at[0], recv_sem=recv.at[0],
            device_id=(grp, peer), device_id_type=MESH,
        )

    def exchange(out, inn, send, recv):
        if not comm:
            inn[...] = out[...]
            return

        for o in range(1, n_sl):
            box_copy(o, out, inn, send, recv).start()

        inn[0] = out[sl]

    def exchange_wait(out, inn, send, recv):
        if not comm:
            return

        boxes = pltpu.make_async_remote_copy(
            src_ref=out.at[pl.ds(1, n_sl - 1)], dst_ref=inn.at[pl.ds(1, n_sl - 1)],
            send_sem=send.at[0], recv_sem=recv.at[0],
            device_id=(grp, lax.rem(sl + 1, n_sl)), device_id_type=MESH,
        )
        boxes.wait_recv()
        boxes.wait_send()

    if comm:
        @pl.when(jnp.logical_not(has_prev))
        def _():
            @pl.loop(1, STEPS + 1)
            def _(t):
                slots[t] = jnp.zeros((4, HALF, GRID), f32)

        pl.semaphore_wait(
            barrier, n_sl - 1 + cross_next.astype(i32) + cross_prev.astype(i32)
        )
    exchange(code_out, code_in, code_send, code_recv)

    def kick(s, field):
        low = jnp.concatenate(
            [
                jnp.concatenate([field[0], field[1]], axis=1),
                jnp.concatenate([field[2], field[3]], axis=1),
            ],
            axis=0,
        ).astype(bf16)
        for j in range(NE // CHUNK):
            lanes = slice(j * CHUNK, (j + 1) * CHUNK)
            picked = mm(low, hot[s, :, lanes]).astype(bf16)
            pick = rhot[s, :, lanes]
            for c in range(2):
                prod = picked[c * HALF:(c + 1) * HALF] * pick
                quad = (prod[0:16] + prod[16:32]) + (prod[32:48] + prod[48:64])
                total = jnp.sum(quad.astype(f32), axis=0, keepdims=True)
                for b in range(CHUNK // EBLK):
                    row = j * (CHUNK // EBLK) + b
                    smp[c, row:row + 1, :] = total[:, b * EBLK:(b + 1) * EBLK]
        energy = ens[s] + kick_gain * (smp[0] * cs[s] - smp[1] * sn[s])
        phase = phs[s] + phase_gain * energy
        ens[s] = energy
        phs[s] = phase
        cs[s] = jnp.cos(phase)
        sn[s] = jnp.sin(phase)

    def emit(s, field):
        for j in range(NBLK):
            lanes = slice(j * EBLK, (j + 1) * EBLK)
            pick = rhot[s, :, lanes]
            spread[0:HALF, lanes] = pick * cs[s, j:j + 1, :].astype(bf16)
            spread[HALF:, lanes] = pick * (-sn[s, j:j + 1, :]).astype(bf16)
        emitted = mm(spread[...], hot_t[s])
        full = jnp.concatenate(
            [
                field[2 * c + h] + emit_gain * emitted[c * HALF:(c + 1) * HALF, h * GRID:(h + 1) * GRID]
                for c in range(2)
                for h in range(2)
            ],
            axis=0,
        )
        high, low = split(full)
        both = jnp.concatenate([high, low], axis=1)
        outs = []
        for h in range(2):
            first = slice(h * HALF, (h + 1) * HALF)
            second = slice(GRID + h * HALF, GRID + (h + 1) * HALF)
            left_hi = jnp.concatenate([lhi_ref[first], lhi_ref[second]], axis=0)
            left_lo = jnp.concatenate([llo_ref[first], llo_ref[second]], axis=0)
            q = mm(left_hi, both)
            half = (mm(left_lo, high) + q[:, GRID:]) + q[:, :GRID]
            wide_hi, wide_lo = split(jnp.concatenate([half[:HALF], half[HALF:]], axis=1))
            q = mm(jnp.concatenate([wide_hi, wide_lo], axis=0), rhi_ref[...])
            outs.append((mm(wide_hi, rlo_ref[...]) + q[HALF:]) + q[:HALF])
        return [outs[h][:, c * GRID:(c + 1) * GRID] for c in range(2) for h in range(2)]

    def slip_copy(t):
        return pltpu.make_async_remote_copy(
            src_ref=sent.at[t], dst_ref=slots.at[t + 1], send_sem=slip_send.at[t],
            recv_sem=slip_recv.at[t], device_id=(next_grp, next_sl), device_id_type=MESH,
        )

    def send_border(t, field):
        for i in range(4):
            sent[t, i] = field[i]
        if comm:
            @pl.when(has_next)
            def _():
                slip_copy(t).start()
        else:
            pltpu.make_async_copy(sent.at[t], slots.at[t + 1], slip_send.at[t]).start()

    def wait_border(t):
        if comm:
            @pl.when(has_prev)
            def _():
                slip_copy(t).wait_recv()
        else:
            pltpu.make_async_copy(sent.at[t], slots.at[t + 1], slip_send.at[t]).wait()

    def load(ref):
        return [ref[i] for i in range(4)]

    @pl.loop(0, STEPS - 1)
    def _(t):
        kick(1, load(cur))
        send_border(t, emit(1, load(cur)))

        @pl.when(t > 0)
        def _():
            wait_border(t - 1)

        kick(0, load(slots.at[t]))
        moved = emit(0, load(slots.at[t]))
        for i in range(4):
            cur[i] = moved[i]

    last = STEPS - 1
    kick(1, load(cur))
    wait_border(last - 1)
    kick(0, load(slots.at[last]))
    final = jnp.concatenate([phs[s] + chicane_r56 * ens[s] for s in range(2)], axis=0)
    weights = jnp.concatenate([jnp.cos(final), -jnp.sin(final)], axis=0).astype(bf16)
    phase_out[...] = mm(place[...], weights).reshape(32, 8, EBLK)
    exchange(phase_out, phase_in, phase_send, phase_recv)

    send_border(last, emit(1, load(cur)))
    moved = emit(0, load(slots.at[last]))
    for c in range(2):
        for h in range(2):
            rad_out[pl.ds(256 + h * 128 + c, HALF, stride=2), :] = moved[2 * c + h]

    exchange_wait(code_out, code_in, code_send, code_recv)

    for p in range(0, 32, 4):
        cells = jnp.concatenate([code_in[p + n] for n in range(4)], axis=0)
        picked = [8 * n + i for n in range(4) for i in range(MOST)]
        transposed_onehots(cells, hot2_t, picked, p * MOST * EBLK)

    exchange_wait(phase_out, phase_in, phase_send, phase_recv)

    for p in range(32):
        for i in range(MOST):
            lanes = slice((p * MOST + i) * EBLK, (p * MOST + i + 1) * EBLK)
            rb = code_in[p, MOST + i:MOST + i + 1, :].astype(bf16)
            here = iota((GRID, EBLK), 0).astype(f32).astype(bf16) == rb
            for c in range(2):
                w = phase_in[p, c * MOST + i:c * MOST + i + 1, :].astype(bf16)
                w = jnp.broadcast_to(w, (GRID, EBLK))
                spread2[c * GRID:(c + 1) * GRID, lanes] = jnp.where(here, w, jnp.zeros_like(w))

    landed = mm(spread2[...], hot2_t[...])
    for c in range(2):
        for s in range(2):
            for h in range(2):
                bun_out[pl.ds(s * 256 + h * 128 + c, HALF, stride=2), :] = landed[
                    c * GRID + s * HALF:c * GRID + (s + 1) * HALF, h * GRID:(h + 1) * GRID
                ]

    wait_border(last)
    for c in range(2):
        for h in range(2):
            rad_out[pl.ds(h * 128 + c, HALF, stride=2), :] = slots[STEPS, 2 * c + h]
    if comm:
        @pl.when(has_next)
        def _():
            @pl.loop(0, STEPS)
            def _(t):
                slip_copy(t).wait_send()


def section(comm, *args):
    vmem = pl.BlockSpec(memory_space=pltpu.VMEM)
    field = (4, HALF, GRID)
    dense = (2, NBLK, EBLK)
    boxes = (32, 2 * MOST, EBLK)
    received = 32 * MOST * EBLK
    dma = pltpu.SemaphoreType.DMA
    return pl.pallas_call(
        functools.partial(kernel, comm),
        out_shape=(jax.ShapeDtypeStruct((512, GRID), f32), jax.ShapeDtypeStruct((512, GRID), f32)),
        in_specs=[pl.BlockSpec(memory_space=pltpu.HBM)] * len(args),
        out_specs=(vmem, vmem),
        scratch_shapes=[
            *[pltpu.VMEM(x.shape, x.dtype) for x in args],
            dma((len(args),)),
            pltpu.VMEM((2, 256, NE), bf16),
            pltpu.VMEM((2, NE, 256), bf16),
            pltpu.VMEM((2, HALF, NE), bf16),
            pltpu.VMEM(dense, i32),
            pltpu.VMEM(dense, i32),
            pltpu.VMEM(dense, f32),
            pltpu.VMEM(dense, f32),
            pltpu.VMEM(dense, f32),
            pltpu.VMEM(dense, f32),
            pltpu.VMEM(dense, f32),
            pltpu.VMEM((2 * HALF, NE), bf16),
            pltpu.VMEM((STEPS + 1,) + field, f32),
            pltpu.VMEM(field, f32),
            pltpu.VMEM((STEPS,) + field, f32),
            pltpu.VMEM((4 * BLK_DEV, 2 * BLK_DEV), bf16),
            pltpu.VMEM(boxes, f32),
            pltpu.VMEM(boxes, f32),
            pltpu.VMEM(boxes, f32),
            pltpu.VMEM(boxes, f32),
            pltpu.VMEM((received, 256), bf16),
            pltpu.VMEM((256, received), bf16),
            dma((STEPS,)),
            dma((STEPS,)),
            dma((1,)),
            dma((1,)),
            dma((1,)),
            dma((1,)),
        ],
        compiler_params=pltpu.CompilerParams(
            collective_id=0 if comm else None, has_side_effects=comm, vmem_limit_bytes=40 << 20
        ),
    )(*[pltpu.with_memory_space_constraint(x, pltpu.HBM) for x in args])


def dense_rows(x):
    return x.reshape(2, NBLK, EBLK).transpose(1, 0, 2).reshape(2 * NBLK, EBLK)


def shards(radiation, phases, energies, cell_row, cell_col, landing, comm=True):
    rad, bun = section(
        comm,
        radiation.reshape(512, GRID),
        dense_rows(phases),
        dense_rows(energies),
        dense_rows(cell_row),
        dense_rows(cell_col),
        landing.reshape(1, BLK_DEV),
        *[jnp.asarray(part) for part in propagator()],
    )
    return rad.reshape(2, GRID, 2, GRID), bun.reshape(2, GRID, 2, GRID)


def solution(mesh):
    both = ("grp", "sl")
    return jax.shard_map(
        shards,
        mesh=mesh,
        in_specs=(
            P(both, None, None, None),
            P(both, None),
            P(both, None),
            P(both, None),
            P(both, None),
            P(both, None),
        ),
        out_specs=(P(both, None, None, None), P(both, None, None, None)),
        check_vma=False,
    )
```

```python
import functools
import math

import jax
import jax.numpy as jnp
import numpy as np
from jax import lax
from jax.experimental import pallas as pl
from jax.experimental.pallas import tpu as pltpu
from jax.sharding import PartitionSpec as P

GRID = 128
HALF = 64
NE = 4096
STEPS = 8
EBLK = 128
NBLK = NE // EBLK
BLK_DEV = 64
MOST = 4
CHUNK = 512

kick_gain = 0.3
phase_gain = 0.5
emit_gain = 1.0
chicane_r56 = 2.0

f32 = jnp.float32
bf16 = jnp.bfloat16
i32 = jnp.int32
MESH = pl.DeviceIdType.MESH


def propagator():
    k = np.arange(GRID)
    kf = np.where(k < GRID - k, k, k - GRID).astype(np.float64)
    o = np.minimum(k, GRID - k)
    turns = (o[:, None] * k[None, :] % GRID).astype(np.float64)
    angles = turns * (2.0 * math.pi / GRID) - 4.0 * math.pi / (GRID * GRID) * (kf * kf)[None, :]
    lag = (k[:, None] - k[None, :]) % GRID
    re = np.cos(angles).mean(axis=1).astype(np.float32)[lag]
    im = np.sin(angles).mean(axis=1).astype(np.float32)[lag]
    left = np.block([[re, -im], [im, re]]).astype(np.float32)
    high = left.astype(bf16)
    low = (left - high.astype(np.float32)).astype(bf16)
    return high, low, np.ascontiguousarray(high.T), np.ascontiguousarray(low.T)


def split(x):
    high = x.astype(bf16)
    return high, (x - high.astype(f32)).astype(bf16)


def cos_sin(x):
    turns = jnp.floor(x * (2.0 / math.pi) + 0.5)
    coarse = jnp.floor(turns * (1.0 / 256.0)) * 256.0
    r = (x - coarse * 1.5703125) - (turns - coarse) * 1.5703125
    r = (r - turns * 4.837512969970703125e-4) - turns * 7.54978995489188216e-8
    z = r * r
    s = ((-1.9515295891e-4 * z + 8.3321608736e-3) * z - 1.6666654611e-1) * z * r + r
    c = (2.443315711809948e-5 * z - 1.388731625493765e-3) * z + 4.166664568298827e-2
    c = c * z * z + (1.0 - 0.5 * z)
    quarter = turns.astype(i32)
    odd = (quarter & 1) == 1
    cos = jnp.where(odd, s, c)
    sin = jnp.where(odd, c, s)
    cos = jnp.where(((quarter + 1) & 2) == 2, -cos, cos)
    sin = jnp.where((quarter & 2) == 2, -sin, sin)
    return cos, sin


def mm(a, b):
    return jnp.dot(a, b, preferred_element_type=f32)


def iota(shape, axis):
    return lax.broadcasted_iota(i32, shape, axis)


def onehot(index, shape, axis):
    places = iota(shape, axis).astype(f32).astype(bf16)
    return jnp.where(places == index, jnp.ones(shape, bf16), jnp.zeros(shape, bf16))


def transposed_onehots(index, out, picked, start):
    turned = index.T
    for n, j in enumerate(picked):
        out[pl.ds(start + n * EBLK, EBLK), :] = onehot(
            turned[:, j:j + 1].astype(bf16), (EBLK, 256), 1
        )


def kernel(
    comm,
    rad_in, ph_in, en_in, row_in, col_in, land_in, lhi_in, llo_in, rhi_in, rlo_in,
    rad_out, bun_out,
    rad_ref, ph_ref, en_ref, row_ref, col_ref, land_ref, lhi_ref, llo_ref, rhi_ref, rlo_ref, in_sem,
    hot, hot_t, rhot, kidx, ridx, phs, ens, cs, sn, smp, spread,
    slots, cur, sent, place,
    code_out, code_in, phase_out, phase_in,
    hot2_t, spread2,
    slip_send, slip_recv, code_send, code_recv, phase_send, phase_recv,
):
    loads = [
        pltpu.make_async_copy(source, target, in_sem.at[n])
        for n, (source, target) in enumerate([
            (row_in, row_ref), (col_in, col_ref), (ph_in, ph_ref), (en_in, en_ref),
            (rad_in, rad_ref), (land_in, land_ref), (lhi_in, lhi_ref), (llo_in, llo_ref),
            (rhi_in, rhi_ref), (rlo_in, rlo_ref),
        ])
    ]
    for one in loads:
        one.start()
    if comm:
        grp = lax.axis_index("grp")
        sl = lax.axis_index("sl")
        n_grp = lax.axis_size("grp")
        n_sl = lax.axis_size("sl")
        has_next = jnp.logical_or(sl < n_sl - 1, grp < n_grp - 1)
        has_prev = jnp.logical_or(sl > 0, grp > 0)
        next_sl = lax.rem(sl + 1, n_sl)
        next_grp = jnp.where(sl == n_sl - 1, jnp.minimum(grp + 1, n_grp - 1), grp)
        prev_sl = lax.rem(sl + n_sl - 1, n_sl)
        prev_grp = jnp.where(sl == 0, jnp.maximum(grp - 1, 0), grp)
        cross_next = jnp.logical_and(sl == n_sl - 1, grp < n_grp - 1)
        cross_prev = jnp.logical_and(sl == 0, grp > 0)
        barrier = pltpu.get_barrier_semaphore()

        for o in range(1, n_sl):
            pl.semaphore_signal(
                barrier, inc=1, device_id=(grp, lax.rem(sl + o, n_sl)), device_id_type=MESH
            )

        @pl.when(cross_next)
        def _():
            pl.semaphore_signal(barrier, inc=1, device_id=(next_grp, next_sl), device_id_type=MESH)

        @pl.when(cross_prev)
        def _():
            pl.semaphore_signal(barrier, inc=1, device_id=(prev_grp, prev_sl), device_id_type=MESH)
    else:
        n_sl = 32

    for one in loads[:2]:
        one.wait()
    for s in range(2):
        rows = row_ref[pl.ds(s, NBLK, stride=2), :]
        cols = col_ref[pl.ds(s, NBLK, stride=2), :]
        kidx[s] = (rows >> 6) * GRID + cols
        ridx[s] = rows & (HALF - 1)
        for j in range(NBLK):
            lanes = slice(j * EBLK, (j + 1) * EBLK)
            kb = kidx[s, j:j + 1, :].astype(f32).astype(bf16)
            rb = ridx[s, j:j + 1, :].astype(f32).astype(bf16)
            hot[s, :, lanes] = onehot(kb, (256, EBLK), 0)
            rhot[s, :, lanes] = onehot(rb, (HALF, EBLK), 0)

        transposed_onehots(kidx[s].astype(f32), hot_t.at[s], range(NBLK), 0)

    for one in loads[2:]:
        one.wait()
    for s in range(2):
        phs[s] = ph_ref[pl.ds(s, NBLK, stride=2), :]
        ens[s] = en_ref[pl.ds(s, NBLK, stride=2), :]
        cs[s], sn[s] = cos_sin(phs[s])
        for c in range(2):
            for h in range(2):
                piece = rad_ref[pl.ds(s * 256 + h * 128 + c, HALF, stride=2), :]
                if s == 0:
                    slots[0, 2 * c + h] = piece
                else:
                    cur[2 * c + h] = piece

    both = 2 * BLK_DEV
    land_row = jnp.broadcast_to(
        jnp.concatenate([land_ref[...], land_ref[...]], axis=1), (both, both)
    )
    first, second = iota((both, both), 0), iota((both, both), 1)
    land_col = jnp.sum(jnp.where(first == second, land_row, 0), axis=1, keepdims=True)
    same = jnp.logical_and(land_col == land_row, first < (second & (BLK_DEV - 1)))
    same = jnp.logical_and(same, first < BLK_DEV)
    earlier = jnp.sum(same.astype(i32), axis=0, keepdims=True)
    slot = land_row[0:1] * MOST + earlier
    box, column = iota((2 * both, both), 0), iota((2 * both, both), 1)
    fits = slot == (box >> 3) * MOST + (box & (MOST - 1))
    fits = jnp.logical_and(fits, ((box >> 2) & 1) == (column >> 6))
    place[...] = fits.astype(f32).astype(bf16)
    cells = jnp.concatenate([kidx[0], kidx[1], ridx[0], ridx[1] + HALF], axis=0)
    code_out[...] = mm(place[...], cells.astype(f32).astype(bf16)).reshape(32, 8, EBLK)

    def box_copy(o, out, inn, send, recv):
        peer = lax.rem(sl + o, n_sl)
        return pltpu.make_async_remote_copy(
            src_ref=out.at[peer], dst_ref=inn.at[o], send_sem=send.at[0], recv_sem=recv.at[0],
            device_id=(grp, peer), device_id_type=MESH,
        )

    def exchange(out, inn, send, recv):
        if not comm:
            inn[...] = out[...]
            return

        for o in range(1, n_sl):
            box_copy(o, out, inn, send, recv).start()

        inn[0] = out[sl]

    def exchange_wait(out, inn, send, recv):
        if not comm:
            return

        boxes = pltpu.make_async_remote_copy(
            src_ref=out.at[pl.ds(1, n_sl - 1)], dst_ref=inn.at[pl.ds(1, n_sl - 1)],
            send_sem=send.at[0], recv_sem=recv.at[0],
            device_id=(grp, lax.rem(sl + 1, n_sl)), device_id_type=MESH,
        )
        boxes.wait_recv()
        boxes.wait_send()

    if comm:
        @pl.when(jnp.logical_not(has_prev))
        def _():
            @pl.loop(1, STEPS + 1)
            def _(t):
                slots[t] = jnp.zeros((4, HALF, GRID), f32)

        pl.semaphore_wait(
            barrier, n_sl - 1 + cross_next.astype(i32) + cross_prev.astype(i32)
        )
    exchange(code_out, code_in, code_send, code_recv)

    def kick(s, field):
        low = jnp.concatenate(
            [
                jnp.concatenate([field[0], field[1]], axis=1),
                jnp.concatenate([field[2], field[3]], axis=1),
            ],
            axis=0,
        ).astype(bf16)
        for j in range(NE // CHUNK):
            lanes = slice(j * CHUNK, (j + 1) * CHUNK)
            picked = mm(low, hot[s, :, lanes]).astype(bf16)
            pick = rhot[s, :, lanes]
            for c in range(2):
                prod = picked[c * HALF:(c + 1) * HALF] * pick
                quad = (prod[0:16] + prod[16:32]) + (prod[32:48] + prod[48:64])
                total = jnp.sum(quad.astype(f32), axis=0, keepdims=True)
                for b in range(CHUNK // EBLK):
                    row = j * (CHUNK // EBLK) + b
                    smp[c, row:row + 1, :] = total[:, b * EBLK:(b + 1) * EBLK]
        energy = ens[s] + kick_gain * (smp[0] * cs[s] - smp[1] * sn[s])
        phase = phs[s] + phase_gain * energy
        ens[s] = energy
        phs[s] = phase
        cs[s], sn[s] = cos_sin(phase)

    def emit(s, field):
        for j in range(NBLK):
            lanes = slice(j * EBLK, (j + 1) * EBLK)
            pick = rhot[s, :, lanes]
            spread[0:HALF, lanes] = pick * cs[s, j:j + 1, :].astype(bf16)
            spread[HALF:, lanes] = pick * (-sn[s, j:j + 1, :]).astype(bf16)
        emitted = mm(spread[...], hot_t[s])
        full = jnp.concatenate(
            [
                field[2 * c + h] + emit_gain * emitted[c * HALF:(c + 1) * HALF, h * GRID:(h + 1) * GRID]
                for c in range(2)
                for h in range(2)
            ],
            axis=0,
        )
        high, low = split(full)
        q = mm(lhi_ref[...], jnp.concatenate([high, low], axis=1))
        half = (mm(llo_ref[...], high) + q[:, GRID:]) + q[:, :GRID]
        high, low = split(jnp.concatenate([half[:GRID], half[GRID:]], axis=1))
        q = mm(jnp.concatenate([high, low], axis=0), rhi_ref[...])
        out = (mm(high, rlo_ref[...]) + q[GRID:]) + q[:GRID]
        return [out[h * HALF:(h + 1) * HALF, c * GRID:(c + 1) * GRID] for c in range(2) for h in range(2)]

    def slip_copy(t):
        return pltpu.make_async_remote_copy(
            src_ref=sent.at[t], dst_ref=slots.at[t + 1], send_sem=slip_send.at[t],
            recv_sem=slip_recv.at[t], device_id=(next_grp, next_sl), device_id_type=MESH,
        )

    def send_border(t, field):
        for i in range(4):
            sent[t, i] = field[i]
        if comm:
            @pl.when(has_next)
            def _():
                slip_copy(t).start()
        else:
            pltpu.make_async_copy(sent.at[t], slots.at[t + 1], slip_send.at[t]).start()

    def wait_border(t):
        if comm:
            @pl.when(has_prev)
            def _():
                slip_copy(t).wait_recv()
        else:
            pltpu.make_async_copy(sent.at[t], slots.at[t + 1], slip_send.at[t]).wait()

    def load(ref):
        return [ref[i] for i in range(4)]

    @pl.loop(0, STEPS - 1)
    def _(t):
        kick(1, load(cur))
        send_border(t, emit(1, load(cur)))

        @pl.when(t > 0)
        def _():
            wait_border(t - 1)

        kick(0, load(slots.at[t]))
        moved = emit(0, load(slots.at[t]))
        for i in range(4):
            cur[i] = moved[i]

    last = STEPS - 1
    kick(1, load(cur))
    wait_border(last - 1)
    kick(0, load(slots.at[last]))
    final = jnp.concatenate([phs[s] + chicane_r56 * ens[s] for s in range(2)], axis=0)
    final_cos, final_sin = cos_sin(final)
    weights = jnp.concatenate([final_cos, -final_sin], axis=0).astype(bf16)
    phase_out[...] = mm(place[...], weights).reshape(32, 8, EBLK)
    exchange(phase_out, phase_in, phase_send, phase_recv)

    send_border(last, emit(1, load(cur)))
    moved = emit(0, load(slots.at[last]))
    for c in range(2):
        for h in range(2):
            rad_out[pl.ds(256 + h * 128 + c, HALF, stride=2), :] = moved[2 * c + h]

    exchange_wait(code_out, code_in, code_send, code_recv)

    for p in range(0, 32, 4):
        cells = jnp.concatenate([code_in[p + n] for n in range(4)], axis=0)
        picked = [8 * n + i for n in range(4) for i in range(MOST)]
        transposed_onehots(cells, hot2_t, picked, p * MOST * EBLK)

    exchange_wait(phase_out, phase_in, phase_send, phase_recv)

    for p in range(32):
        for i in range(MOST):
            lanes = slice((p * MOST + i) * EBLK, (p * MOST + i + 1) * EBLK)
            rb = code_in[p, MOST + i:MOST + i + 1, :].astype(bf16)
            here = iota((GRID, EBLK), 0).astype(f32).astype(bf16) == rb
            for c in range(2):
                w = phase_in[p, c * MOST + i:c * MOST + i + 1, :].astype(bf16)
                w = jnp.broadcast_to(w, (GRID, EBLK))
                spread2[c * GRID:(c + 1) * GRID, lanes] = jnp.where(here, w, jnp.zeros_like(w))

    landed = mm(spread2[...], hot2_t[...])
    for c in range(2):
        for s in range(2):
            for h in range(2):
                bun_out[pl.ds(s * 256 + h * 128 + c, HALF, stride=2), :] = landed[
                    c * GRID + s * HALF:c * GRID + (s + 1) * HALF, h * GRID:(h + 1) * GRID
                ]

    wait_border(last)
    for c in range(2):
        for h in range(2):
            rad_out[pl.ds(h * 128 + c, HALF, stride=2), :] = slots[STEPS, 2 * c + h]
    if comm:
        @pl.when(has_next)
        def _():
            @pl.loop(0, STEPS)
            def _(t):
                slip_copy(t).wait_send()


def section(comm, *args):
    vmem = pl.BlockSpec(memory_space=pltpu.VMEM)
    field = (4, HALF, GRID)
    dense = (2, NBLK, EBLK)
    boxes = (32, 2 * MOST, EBLK)
    received = 32 * MOST * EBLK
    dma = pltpu.SemaphoreType.DMA
    return pl.pallas_call(
        functools.partial(kernel, comm),
        out_shape=(jax.ShapeDtypeStruct((512, GRID), f32), jax.ShapeDtypeStruct((512, GRID), f32)),
        in_specs=[pl.BlockSpec(memory_space=pltpu.HBM)] * len(args),
        out_specs=(vmem, vmem),
        scratch_shapes=[
            *[pltpu.VMEM(x.shape, x.dtype) for x in args],
            dma((len(args),)),
            pltpu.VMEM((2, 256, NE), bf16),
            pltpu.VMEM((2, NE, 256), bf16),
            pltpu.VMEM((2, HALF, NE), bf16),
            pltpu.VMEM(dense, i32),
            pltpu.VMEM(dense, i32),
            pltpu.VMEM(dense, f32),
            pltpu.VMEM(dense, f32),
            pltpu.VMEM(dense, f32),
            pltpu.VMEM(dense, f32),
            pltpu.VMEM(dense, f32),
            pltpu.VMEM((2 * HALF, NE), bf16),
            pltpu.VMEM((STEPS + 1,) + field, f32),
            pltpu.VMEM(field, f32),
            pltpu.VMEM((STEPS,) + field, f32),
            pltpu.VMEM((4 * BLK_DEV, 2 * BLK_DEV), bf16),
            pltpu.VMEM(boxes, f32),
            pltpu.VMEM(boxes, f32),
            pltpu.VMEM(boxes, f32),
            pltpu.VMEM(boxes, f32),
            pltpu.VMEM((received, 256), bf16),
            pltpu.VMEM((256, received), bf16),
            dma((STEPS,)),
            dma((STEPS,)),
            dma((1,)),
            dma((1,)),
            dma((1,)),
            dma((1,)),
        ],
        compiler_params=pltpu.CompilerParams(
            collective_id=0 if comm else None, has_side_effects=comm, vmem_limit_bytes=40 << 20
        ),
    )(*[pltpu.with_memory_space_constraint(x, pltpu.HBM) for x in args])


def dense_rows(x):
    return x.reshape(2, NBLK, EBLK).transpose(1, 0, 2).reshape(2 * NBLK, EBLK)


def shards(radiation, phases, energies, cell_row, cell_col, landing, comm=True):
    rad, bun = section(
        comm,
        radiation.reshape(512, GRID),
        dense_rows(phases),
        dense_rows(energies),
        dense_rows(cell_row),
        dense_rows(cell_col),
        landing.reshape(1, BLK_DEV),
        *[jnp.asarray(part) for part in propagator()],
    )
    return rad.reshape(2, GRID, 2, GRID), bun.reshape(2, GRID, 2, GRID)


def solution(mesh):
    both = ("grp", "sl")
    return jax.shard_map(
        shards,
        mesh=mesh,
        in_specs=(
            P(both, None, None, None),
            P(both, None),
            P(both, None),
            P(both, None),
            P(both, None),
            P(both, None),
        ),
        out_specs=(P(both, None, None, None), P(both, None, None, None)),
        check_vma=False,
    )
```

```python
import functools
import math

import jax
import jax.numpy as jnp
import numpy as np
from jax import lax
from jax.experimental import pallas as pl
from jax.experimental.pallas import tpu as pltpu
from jax.sharding import PartitionSpec as P

GRID = 128
HALF = 64
NE = 4096
STEPS = 8
EBLK = 128
NBLK = NE // EBLK
BLK_DEV = 64
MOST = 4
CHUNK = 512

kick_gain = 0.3
phase_gain = 0.5
emit_gain = 1.0
chicane_r56 = 2.0

f32 = jnp.float32
bf16 = jnp.bfloat16
i32 = jnp.int32
MESH = pl.DeviceIdType.MESH


def propagator():
    k = np.arange(GRID)
    kf = np.where(k < GRID - k, k, k - GRID).astype(np.float64)
    o = np.minimum(k, GRID - k)
    turns = (o[:, None] * k[None, :] % GRID).astype(np.float64)
    angles = turns * (2.0 * math.pi / GRID) - 4.0 * math.pi / (GRID * GRID) * (kf * kf)[None, :]
    lag = (k[:, None] - k[None, :]) % GRID
    re = np.cos(angles).mean(axis=1).astype(np.float32)[lag]
    im = np.sin(angles).mean(axis=1).astype(np.float32)[lag]
    left = np.block([[re, -im], [im, re]]).astype(np.float32)
    high = left.astype(bf16)
    low = (left - high.astype(np.float32)).astype(bf16)
    return high, low, np.ascontiguousarray(high.T), np.ascontiguousarray(low.T)


def split(x):
    high = x.astype(bf16)
    return high, (x - high.astype(f32)).astype(bf16)


def cos_sin(x):
    turns = jnp.floor(x * (2.0 / math.pi) + 0.5)
    coarse = jnp.floor(turns * (1.0 / 256.0) + 0.5) * 256.0
    r = (x - coarse * 1.5703125) - (turns - coarse) * 1.5703125
    r = (r - turns * 4.837512969970703125e-4) - turns * 7.54978995489188216e-8
    z = r * r
    s = ((-1.9515295891e-4 * z + 8.3321608736e-3) * z - 1.6666654611e-1) * z * r + r
    c = (2.443315711809948e-5 * z - 1.388731625493765e-3) * z + 4.166664568298827e-2
    c = c * z * z + (1.0 - 0.5 * z)
    quarter = turns.astype(i32)
    odd = (quarter & 1) == 1
    cos = jnp.where(odd, s, c)
    sin = jnp.where(odd, c, s)
    cos = jnp.where(((quarter + 1) & 2) == 2, -cos, cos)
    sin = jnp.where((quarter & 2) == 2, -sin, sin)
    return cos, sin


def mm(a, b):
    return jnp.dot(a, b, preferred_element_type=f32)


def iota(shape, axis):
    return lax.broadcasted_iota(i32, shape, axis)


def onehot(index, shape, axis):
    places = iota(shape, axis).astype(f32).astype(bf16)
    return jnp.where(places == index, jnp.ones(shape, bf16), jnp.zeros(shape, bf16))


def transposed_onehots(index, out, picked, start):
    turned = index.T
    for n, j in enumerate(picked):
        out[pl.ds(start + n * EBLK, EBLK), :] = onehot(
            turned[:, j:j + 1].astype(bf16), (EBLK, 256), 1
        )


def kernel(
    comm,
    rad_in, ph_in, en_in, row_in, col_in, land_in, lhi_in, llo_in, rhi_in, rlo_in,
    rad_out, bun_out,
    rad_ref, ph_ref, en_ref, row_ref, col_ref, land_ref, lhi_ref, llo_ref, rhi_ref, rlo_ref, in_sem,
    hot, hot_t, rhot, kidx, ridx, phs, ens, cs, sn, smp, spread,
    slots, cur, sent, place,
    code_out, code_in, phase_out, phase_in,
    hot2_t, spread2,
    slip_send, slip_recv, code_send, code_recv, phase_send, phase_recv,
):
    loads = [
        pltpu.make_async_copy(source, target, in_sem.at[n])
        for n, (source, target) in enumerate([
            (row_in, row_ref), (col_in, col_ref), (ph_in, ph_ref), (en_in, en_ref),
            (rad_in, rad_ref), (land_in, land_ref), (lhi_in, lhi_ref), (llo_in, llo_ref),
            (rhi_in, rhi_ref), (rlo_in, rlo_ref),
        ])
    ]
    for one in loads:
        one.start()
    if comm:
        grp = lax.axis_index("grp")
        sl = lax.axis_index("sl")
        n_grp = lax.axis_size("grp")
        n_sl = lax.axis_size("sl")
        has_next = jnp.logical_or(sl < n_sl - 1, grp < n_grp - 1)
        has_prev = jnp.logical_or(sl > 0, grp > 0)
        next_sl = lax.rem(sl + 1, n_sl)
        next_grp = jnp.where(sl == n_sl - 1, jnp.minimum(grp + 1, n_grp - 1), grp)
        prev_sl = lax.rem(sl + n_sl - 1, n_sl)
        prev_grp = jnp.where(sl == 0, jnp.maximum(grp - 1, 0), grp)
        cross_next = jnp.logical_and(sl == n_sl - 1, grp < n_grp - 1)
        cross_prev = jnp.logical_and(sl == 0, grp > 0)
        barrier = pltpu.get_barrier_semaphore()

        for o in range(1, n_sl):
            pl.semaphore_signal(
                barrier, inc=1, device_id=(grp, lax.rem(sl + o, n_sl)), device_id_type=MESH
            )

        @pl.when(cross_next)
        def _():
            pl.semaphore_signal(barrier, inc=1, device_id=(next_grp, next_sl), device_id_type=MESH)

        @pl.when(cross_prev)
        def _():
            pl.semaphore_signal(barrier, inc=1, device_id=(prev_grp, prev_sl), device_id_type=MESH)
    else:
        n_sl = 32

    for one in loads[:2]:
        one.wait()
    for s in range(2):
        rows = row_ref[pl.ds(s, NBLK, stride=2), :]
        cols = col_ref[pl.ds(s, NBLK, stride=2), :]
        kidx[s] = (rows >> 6) * GRID + cols
        ridx[s] = rows & (HALF - 1)
        for j in range(NBLK):
            lanes = slice(j * EBLK, (j + 1) * EBLK)
            kb = kidx[s, j:j + 1, :].astype(f32).astype(bf16)
            rb = ridx[s, j:j + 1, :].astype(f32).astype(bf16)
            hot[s, :, lanes] = onehot(kb, (256, EBLK), 0)
            rhot[s, :, lanes] = onehot(rb, (HALF, EBLK), 0)

        transposed_onehots(kidx[s].astype(f32), hot_t.at[s], range(NBLK), 0)

    for one in loads[2:]:
        one.wait()
    for s in range(2):
        phs[s] = ph_ref[pl.ds(s, NBLK, stride=2), :]
        ens[s] = en_ref[pl.ds(s, NBLK, stride=2), :]
        cs[s], sn[s] = cos_sin(phs[s])
        for c in range(2):
            for h in range(2):
                piece = rad_ref[pl.ds(s * 256 + h * 128 + c, HALF, stride=2), :]
                if s == 0:
                    slots[0, 2 * c + h] = piece
                else:
                    cur[2 * c + h] = piece

    both = 2 * BLK_DEV
    land_row = jnp.broadcast_to(
        jnp.concatenate([land_ref[...], land_ref[...]], axis=1), (both, both)
    )
    first, second = iota((both, both), 0), iota((both, both), 1)
    land_col = jnp.sum(jnp.where(first == second, land_row, 0), axis=1, keepdims=True)
    same = jnp.logical_and(land_col == land_row, first < (second & (BLK_DEV - 1)))
    same = jnp.logical_and(same, first < BLK_DEV)
    earlier = jnp.sum(same.astype(i32), axis=0, keepdims=True)
    slot = land_row[0:1] * MOST + earlier
    box, column = iota((2 * both, both), 0), iota((2 * both, both), 1)
    fits = slot == (box >> 3) * MOST + (box & (MOST - 1))
    fits = jnp.logical_and(fits, ((box >> 2) & 1) == (column >> 6))
    place[...] = fits.astype(f32).astype(bf16)
    cells = jnp.concatenate([kidx[0], kidx[1], ridx[0], ridx[1] + HALF], axis=0)
    code_out[...] = mm(place[...], cells.astype(f32).astype(bf16)).reshape(32, 8, EBLK)

    def box_copy(o, out, inn, send, recv):
        peer = lax.rem(sl + o, n_sl)
        return pltpu.make_async_remote_copy(
            src_ref=out.at[peer], dst_ref=inn.at[o], send_sem=send.at[0], recv_sem=recv.at[0],
            device_id=(grp, peer), device_id_type=MESH,
        )

    def exchange(out, inn, send, recv):
        if not comm:
            inn[...] = out[...]
            return

        for o in range(1, n_sl):
            box_copy(o, out, inn, send, recv).start()

        inn[0] = out[sl]

    def exchange_wait(out, inn, send, recv):
        if not comm:
            return

        boxes = pltpu.make_async_remote_copy(
            src_ref=out.at[pl.ds(1, n_sl - 1)], dst_ref=inn.at[pl.ds(1, n_sl - 1)],
            send_sem=send.at[0], recv_sem=recv.at[0],
            device_id=(grp, lax.rem(sl + 1, n_sl)), device_id_type=MESH,
        )
        boxes.wait_recv()
        boxes.wait_send()

    if comm:
        @pl.when(jnp.logical_not(has_prev))
        def _():
            @pl.loop(1, STEPS + 1)
            def _(t):
                slots[t] = jnp.zeros((4, HALF, GRID), f32)

        pl.semaphore_wait(
            barrier, n_sl - 1 + cross_next.astype(i32) + cross_prev.astype(i32)
        )
    exchange(code_out, code_in, code_send, code_recv)

    def kick(s, field):
        low = jnp.concatenate(
            [
                jnp.concatenate([field[0], field[1]], axis=1),
                jnp.concatenate([field[2], field[3]], axis=1),
            ],
            axis=0,
        ).astype(bf16)
        for j in range(NE // CHUNK):
            lanes = slice(j * CHUNK, (j + 1) * CHUNK)
            picked = mm(low, hot[s, :, lanes]).astype(bf16)
            pick = rhot[s, :, lanes]
            for c in range(2):
                prod = picked[c * HALF:(c + 1) * HALF] * pick
                quad = (prod[0:16] + prod[16:32]) + (prod[32:48] + prod[48:64])
                total = jnp.sum(quad.astype(f32), axis=0, keepdims=True)
                for b in range(CHUNK // EBLK):
                    row = j * (CHUNK // EBLK) + b
                    smp[c, row:row + 1, :] = total[:, b * EBLK:(b + 1) * EBLK]
        energy = ens[s] + kick_gain * (smp[0] * cs[s] - smp[1] * sn[s])
        phase = phs[s] + phase_gain * energy
        ens[s] = energy
        phs[s] = phase
        cs[s], sn[s] = cos_sin(phase)

    def emit(s, field):
        for j in range(NBLK):
            lanes = slice(j * EBLK, (j + 1) * EBLK)
            pick = rhot[s, :, lanes]
            spread[0:HALF, lanes] = pick * cs[s, j:j + 1, :].astype(bf16)
            spread[HALF:, lanes] = pick * (-sn[s, j:j + 1, :]).astype(bf16)
        emitted = mm(spread[...], hot_t[s])
        full = jnp.concatenate(
            [
                field[2 * c + h] + emit_gain * emitted[c * HALF:(c + 1) * HALF, h * GRID:(h + 1) * GRID]
                for c in range(2)
                for h in range(2)
            ],
            axis=0,
        )
        high, low = split(full)
        q = mm(lhi_ref[...], jnp.concatenate([high, low], axis=1))
        half = (mm(llo_ref[...], high) + q[:, GRID:]) + q[:, :GRID]
        high, low = split(jnp.concatenate([half[:GRID], half[GRID:]], axis=1))
        q = mm(jnp.concatenate([high, low], axis=0), rhi_ref[...])
        out = (mm(high, rlo_ref[...]) + q[GRID:]) + q[:GRID]
        return [out[h * HALF:(h + 1) * HALF, c * GRID:(c + 1) * GRID] for c in range(2) for h in range(2)]

    def slip_copy(t):
        return pltpu.make_async_remote_copy(
            src_ref=sent.at[t], dst_ref=slots.at[t + 1], send_sem=slip_send.at[t],
            recv_sem=slip_recv.at[t], device_id=(next_grp, next_sl), device_id_type=MESH,
        )

    def send_border(t, field):
        for i in range(4):
            sent[t, i] = field[i]
        if comm:
            @pl.when(has_next)
            def _():
                slip_copy(t).start()
        else:
            pltpu.make_async_copy(sent.at[t], slots.at[t + 1], slip_send.at[t]).start()

    def wait_border(t):
        if comm:
            @pl.when(has_prev)
            def _():
                slip_copy(t).wait_recv()
        else:
            pltpu.make_async_copy(sent.at[t], slots.at[t + 1], slip_send.at[t]).wait()

    def load(ref):
        return [ref[i] for i in range(4)]

    @pl.loop(0, STEPS - 1)
    def _(t):
        kick(1, load(cur))
        send_border(t, emit(1, load(cur)))

        @pl.when(t > 0)
        def _():
            wait_border(t - 1)

        kick(0, load(slots.at[t]))
        moved = emit(0, load(slots.at[t]))
        for i in range(4):
            cur[i] = moved[i]

    last = STEPS - 1
    kick(1, load(cur))
    wait_border(last - 1)
    kick(0, load(slots.at[last]))
    final = jnp.concatenate([phs[s] + chicane_r56 * ens[s] for s in range(2)], axis=0)
    final_cos, final_sin = cos_sin(final)
    weights = jnp.concatenate([final_cos, -final_sin], axis=0).astype(bf16)
    phase_out[...] = mm(place[...], weights).reshape(32, 8, EBLK)
    exchange(phase_out, phase_in, phase_send, phase_recv)

    send_border(last, emit(1, load(cur)))
    moved = emit(0, load(slots.at[last]))
    for c in range(2):
        for h in range(2):
            rad_out[pl.ds(256 + h * 128 + c, HALF, stride=2), :] = moved[2 * c + h]

    exchange_wait(code_out, code_in, code_send, code_recv)

    for p in range(0, 32, 4):
        cells = jnp.concatenate([code_in[p + n] for n in range(4)], axis=0)
        picked = [8 * n + i for n in range(4) for i in range(MOST)]
        transposed_onehots(cells, hot2_t, picked, p * MOST * EBLK)

    exchange_wait(phase_out, phase_in, phase_send, phase_recv)

    for p in range(32):
        for i in range(MOST):
            lanes = slice((p * MOST + i) * EBLK, (p * MOST + i + 1) * EBLK)
            rb = code_in[p, MOST + i:MOST + i + 1, :].astype(bf16)
            here = iota((GRID, EBLK), 0).astype(f32).astype(bf16) == rb
            for c in range(2):
                w = phase_in[p, c * MOST + i:c * MOST + i + 1, :].astype(bf16)
                w = jnp.broadcast_to(w, (GRID, EBLK))
                spread2[c * GRID:(c + 1) * GRID, lanes] = jnp.where(here, w, jnp.zeros_like(w))

    landed = mm(spread2[...], hot2_t[...])
    for c in range(2):
        for s in range(2):
            for h in range(2):
                bun_out[pl.ds(s * 256 + h * 128 + c, HALF, stride=2), :] = landed[
                    c * GRID + s * HALF:c * GRID + (s + 1) * HALF, h * GRID:(h + 1) * GRID
                ]

    wait_border(last)
    for c in range(2):
        for h in range(2):
            rad_out[pl.ds(h * 128 + c, HALF, stride=2), :] = slots[STEPS, 2 * c + h]
    if comm:
        @pl.when(has_next)
        def _():
            @pl.loop(0, STEPS)
            def _(t):
                slip_copy(t).wait_send()


def section(comm, *args):
    vmem = pl.BlockSpec(memory_space=pltpu.VMEM)
    field = (4, HALF, GRID)
    dense = (2, NBLK, EBLK)
    boxes = (32, 2 * MOST, EBLK)
    received = 32 * MOST * EBLK
    dma = pltpu.SemaphoreType.DMA
    return pl.pallas_call(
        functools.partial(kernel, comm),
        out_shape=(jax.ShapeDtypeStruct((512, GRID), f32), jax.ShapeDtypeStruct((512, GRID), f32)),
        in_specs=[pl.BlockSpec(memory_space=pltpu.HBM)] * len(args),
        out_specs=(vmem, vmem),
        scratch_shapes=[
            *[pltpu.VMEM(x.shape, x.dtype) for x in args],
            dma((len(args),)),
            pltpu.VMEM((2, 256, NE), bf16),
            pltpu.VMEM((2, NE, 256), bf16),
            pltpu.VMEM((2, HALF, NE), bf16),
            pltpu.VMEM(dense, i32),
            pltpu.VMEM(dense, i32),
            pltpu.VMEM(dense, f32),
            pltpu.VMEM(dense, f32),
            pltpu.VMEM(dense, f32),
            pltpu.VMEM(dense, f32),
            pltpu.VMEM(dense, f32),
            pltpu.VMEM((2 * HALF, NE), bf16),
            pltpu.VMEM((STEPS + 1,) + field, f32),
            pltpu.VMEM(field, f32),
            pltpu.VMEM((STEPS,) + field, f32),
            pltpu.VMEM((4 * BLK_DEV, 2 * BLK_DEV), bf16),
            pltpu.VMEM(boxes, f32),
            pltpu.VMEM(boxes, f32),
            pltpu.VMEM(boxes, f32),
            pltpu.VMEM(boxes, f32),
            pltpu.VMEM((received, 256), bf16),
            pltpu.VMEM((256, received), bf16),
            dma((STEPS,)),
            dma((STEPS,)),
            dma((1,)),
            dma((1,)),
            dma((1,)),
            dma((1,)),
        ],
        compiler_params=pltpu.CompilerParams(
            collective_id=0 if comm else None, has_side_effects=comm, vmem_limit_bytes=40 << 20
        ),
    )(*[pltpu.with_memory_space_constraint(x, pltpu.HBM) for x in args])


def dense_rows(x):
    return x.reshape(2, NBLK, EBLK).transpose(1, 0, 2).reshape(2 * NBLK, EBLK)


def shards(radiation, phases, energies, cell_row, cell_col, landing, comm=True):
    rad, bun = section(
        comm,
        radiation.reshape(512, GRID),
        dense_rows(phases),
        dense_rows(energies),
        dense_rows(cell_row),
        dense_rows(cell_col),
        landing.reshape(1, BLK_DEV),
        *[jnp.asarray(part) for part in propagator()],
    )
    return rad.reshape(2, GRID, 2, GRID), bun.reshape(2, GRID, 2, GRID)


def solution(mesh):
    both = ("grp", "sl")
    return jax.shard_map(
        shards,
        mesh=mesh,
        in_specs=(
            P(both, None, None, None),
            P(both, None),
            P(both, None),
            P(both, None),
            P(both, None),
            P(both, None),
        ),
        out_specs=(P(both, None, None, None), P(both, None, None, None)),
        check_vma=False,
    )
```
